256 devices in a mesh: pop: 16 (over z_hi, x, core), shard: 16 (over y, z_lo).
Axes of the slice: x: 4, y: 4, z: 8 (z_hi: 2, z_lo: 4; z = z_hi * 4 + z_lo), core: 2. Of those that a mesh axis runs over, the one named last changes fastest.
Arguments:
- tokens: bfloat16 [32, 480, 4096], P('pop'), may hold values from -6 to 6
- gate_weight_matrix: bfloat16 [4096, 14336], P('pop', 'shard'), may hold values from -0.09375 to 0.09375
- w_up: bfloat16 [4096, 14336], P('pop', 'shard'), may hold values from -0.09375 to 0.09375
- a_gate: bfloat16 [32, 4, 4096], P('pop'), may hold values from -5 to 5
- a_up: bfloat16 [32, 4, 4096], P('pop'), may hold values from -5 to 5
- gate_hidden_factors: bfloat16 [32, 4, 14336], P('pop', None, 'shard'), may hold values from -5 to 5
- up_hidden_factors: bfloat16 [32, 4, 14336], P('pop', None, 'shard'), may hold values from -5 to 5
- fitness: bfloat16 [32], P('pop'), may hold values from -1 to 1
- readout: float32 [14336], P('shard'), may hold values from -0.13363062 to 0.13363062
Outputs:
- scores: float32 [32, 480], P('pop')
- upd_gate: float32 [4096, 14336], P('pop', 'shard')
- up_update_direction: float32 [4096, 14336], P('pop', 'shard')
The draws below stay inside these ranges and needn't reach their ends.
All inputs are finite; a program needn't handle non-finite values.
Results may differ from the reference program's by a relative error of at most 0.0003.
Values may be sent and summed in bfloat16 or wider, within the bound.
A program may use at most 128 MiB of HBM per device.

```python
import math
import jax
import jax.numpy as jnp
from jax import lax

D = 4096
F = 14336
RANK = 4
TOK = 480
MEMBERS = 32


def draw_readout(key, part):
    position = jnp.arange(F, dtype=jnp.float32) / F
    values = jnp.clip(jax.random.normal(key, (F,), jnp.float32), -4.0, 4.0) * jnp.power(3.0, position)
    return values / math.sqrt(F)


def levels(own_key, extent, cuts, least, high):
    gain = 1.0
    for axis_at, blocks in cuts:
        steps = jax.random.uniform(jax.random.fold_in(jax.random.fold_in(own_key, 6), axis_at), (blocks,), jnp.float32, least / len(cuts), high / len(cuts))
        gain = gain * jnp.repeat(jnp.exp(steps), extent[axis_at] // blocks).reshape((-1,) + (1,) * (len(extent) - 1 - axis_at))
    return gain


def gaussian(rng, extent, deviation, limit, cuts=(), held_as=jnp.bfloat16):
    factor_of = levels(rng, extent, cuts, -0.22, 0.18) if cuts else 1.0
    array = jax.random.normal(rng, extent, jnp.float32) * deviation * factor_of
    return jnp.minimum(jnp.maximum(array, -limit), limit).astype(held_as)


def setup_inputs(seed: int = 0) -> dict:
    streams_of = jax.random.split(jax.random.key(seed), 10)
    tokens = gaussian(streams_of[0], (MEMBERS, TOK, D), 1.0, 6.0, ((0, 16),))
    gate_weight_matrix = gaussian(streams_of[1], (D, F), D ** -0.5, 0.09375, ((0, 16), (1, 16)))
    w_up = gaussian(streams_of[2], (D, F), D ** -0.5, 0.09375, ((0, 16), (1, 16)))
    a_gate = gaussian(streams_of[3], (MEMBERS, RANK, D), 1.0, 5.0, ((0, 16),))
    a_up = gaussian(streams_of[4], (MEMBERS, RANK, D), 1.0, 5.0, ((0, 16),))
    gate_hidden_factors = gaussian(streams_of[5], (MEMBERS, RANK, F), 1.0, 5.0, ((0, 16), (2, 16)))
    up_hidden_factors = gaussian(streams_of[6], (MEMBERS, RANK, F), 1.0, 5.0, ((0, 16), (2, 16)))
    fitness = jnp.clip(jax.random.uniform(streams_of[7], (MEMBERS,), jnp.float32, -1.0, 1.0) * levels(streams_of[7], (MEMBERS,), ((0, 16),), -0.4, 0.0), -1.0, 1.0).astype(jnp.bfloat16)
    readout = draw_readout(jax.random.fold_in(streams_of[9], 71), 0)
    return dict(tokens=tokens, gate_weight_matrix=gate_weight_matrix, w_up=w_up, a_gate=a_gate, a_up=a_up, gate_hidden_factors=gate_hidden_factors, up_hidden_factors=up_hidden_factors, fitness=fitness, readout=readout)


def member_fitness_eval(operands, gate_weight_matrix, w_up, readout, noise_scale):
    member_tokens, row_gate, row_up, col_gate, col_up = operands
    gate_projected = jnp.dot(member_tokens, row_gate.T, preferred_element_type=jnp.float32)
    up_projected = jnp.dot(member_tokens, row_up.T, preferred_element_type=jnp.float32)
    gate_pre = jnp.dot(member_tokens, gate_weight_matrix, preferred_element_type=jnp.float32) + noise_scale * jnp.dot(gate_projected, col_gate.astype(jnp.float32), precision=lax.Precision.HIGHEST)
    up_pre = jnp.dot(member_tokens, w_up, preferred_element_type=jnp.float32) + noise_scale * jnp.dot(up_projected, col_up.astype(jnp.float32), precision=lax.Precision.HIGHEST)
    hidden = jax.nn.silu(gate_pre) * up_pre
    return jnp.dot(hidden, readout, precision=lax.Precision.HIGHEST)

def direction(row_factor, col_factor, weighting):
    left_side = (row_factor.astype(jnp.float32) * weighting[:, None, None]).reshape(-1, row_factor.shape[2])
    right_side = col_factor.astype(jnp.float32).reshape(-1, col_factor.shape[2])
    return lax.dot_general(left_side, right_side, (((0,), (0,)), ((), ())), precision=lax.Precision.HIGHEST)

def reference(tokens, gate_weight_matrix, w_up, a_gate, a_up, gate_hidden_factors, up_hidden_factors, fitness, readout):
    noise_scale = 0.25 / math.sqrt(D * RANK)
    scores = lax.map(lambda operands: member_fitness_eval(operands, gate_weight_matrix, w_up, readout, noise_scale), (tokens, a_gate, a_up, gate_hidden_factors, up_hidden_factors))
    weighting = fitness.astype(jnp.float32) / math.sqrt(MEMBERS * RANK)
    upd_gate = direction(a_gate, gate_hidden_factors, weighting)
    up_update_direction = direction(a_up, up_hidden_factors, weighting)
    return (scores, upd_gate, up_update_direction)
```

```python
import functools
import math

import jax
import jax.numpy as jnp
from jax import lax
from jax.experimental import pallas as pl
from jax.experimental.pallas import tpu as pltpu
from jax.sharding import PartitionSpec as P

MESH = pl.DeviceIdType.MESH
F32 = jnp.float32
BF16 = jnp.bfloat16
LANES = 128
RING = 4
CORES = 2
SMALL = 16
(Z, A_LO, A_HI, B_LO, B_HI, RA_LO, RA_HI, RB_LO, RB_HI,
 S_OWN, S_Z, S_A_LO, S_A_HI, S_B_LO, S_B_HI, S_RA, S_RB) = range(17)
KINDS = 17


def dot(a, b, dims=((1,), (0,)), precision=None):
    return lax.dot_general(a, b, (dims, ((), ())), precision=precision, preferred_element_type=F32)


def kernel(
    noise, out_scale, n_pop, n_shard,
    tok_hbm, wg_hbm, wu_hbm, ag_hbm, au_hbm, hg_hbm, hu_hbm, fit_ref, ro_ref,
    sc_ref, ug_hbm, uu_hbm,
    tok, gath, acc, total, ext, fac, ag, au, hg, hu, msg, abuf, left, stage, parts,
    send, recv, wsem, lsem, asend, arecv, bsend, brecv, psend, precv, osem,
):
    pop, sh = lax.axis_index("pop"), lax.axis_index("shard")
    core, chip = pop % CORES, pop // CORES
    x, zh = chip % RING, chip // RING
    chunks = gath.shape[0]
    depth = wg_hbm.shape[0]
    rows = tok.shape[0]
    members = tok_hbm.shape[0]
    per_member = rows // members
    block = 2 * depth + SMALL
    first = depth + SMALL
    span = CORES * depth

    def at(dx, dz):
        return (zh + dz) % 2 * RING + (x + dx) % RING

    def dev(c, k):
        return (c * CORES + k, sh)

    own, zown = at(0, 0), at(0, 1)
    xp, xm, xx = at(1, 0), at(3, 0), at(2, 0)
    zp, zm, zx = at(1, 1), at(3, 1), at(2, 1)

    barrier = pltpu.get_barrier_semaphore()

    @pl.loop(1, n_pop)
    def _(d):
        pl.semaphore_signal(barrier, inc=1, device_id=((pop + d) % n_pop, sh), device_id_type=MESH)

    @pl.loop(1, n_shard)
    def _(d):
        pl.semaphore_signal(barrier, inc=1, device_id=(pop, (sh + d) % n_shard), device_id_type=MESH)

    def weight_load(t, k):
        src = (wg_hbm, wu_hbm)[k]
        col = pl.multiple_of(t * LANES, LANES)
        return pltpu.make_async_copy(
            src.at[:, pl.ds(col, LANES)], gath.at[t, own, core, pl.ds(k * depth, depth)], wsem.at[k, t]
        )

    small_loads = [
        pltpu.make_async_copy(a, b, lsem.at[i])
        for i, (a, b) in enumerate(((hg_hbm, hg), (hu_hbm, hu), (ag_hbm, ag), (au_hbm, au)))
    ]
    tok_loads = [
        pltpu.make_async_copy(
            tok_hbm.at[m], tok.at[pl.ds(m * per_member, per_member)], lsem.at[4 + m]
        )
        for m in range(members)
    ]
    for c in small_loads:
        c.start()

    @pl.loop(0, chunks)
    def _(t):
        weight_load(t, 0).start()
        weight_load(t, 1).start()

    for c in tok_loads:
        c.start()

    for c in small_loads[:2]:
        c.wait()

    def pack(gate, up):
        return jnp.concatenate(
            [gate[0].astype(F32), gate[1].astype(F32), up[0].astype(F32), up[1].astype(F32)], axis=0
        ).astype(BF16)

    factors = pack(hg, hu)
    for t in range(chunks):
        gath[t, own, core, 2 * depth:, :] = factors[:, t * LANES:(t + 1) * LANES]

    @pl.loop(0, chunks)
    def _(t):
        weight_load(t, 0).wait()
        weight_load(t, 1).wait()

    pl.semaphore_wait(barrier, n_pop - 1 + n_shard - 1)

    def remote(kind, t, c, k, target, lo=0, n=block):
        ref = gath.at[t, c, k, pl.ds(lo, n)]
        return pltpu.make_async_remote_copy(
            src_ref=ref, dst_ref=ref, send_sem=send.at[kind, t], recv_sem=recv.at[kind, t],
            device_id=target, device_id_type=MESH,
        )

    to_z, to_p, to_m, to_s = dev(zown, core), dev(xp, core), dev(xm, core), dev(own, 1 - core)
    second = block - first

    sends = {
        Z: (own, 0, block, to_z),
        A_LO: (own, 0, block, to_p), A_HI: (own, 0, block, to_m),
        B_LO: (zown, 0, block, to_p), B_HI: (zown, 0, block, to_m),
        RA_LO: (xm, 0, first, to_p), RA_HI: (xp, first, second, to_m),
        RB_LO: (zm, first, second, to_p), RB_HI: (zp, 0, first, to_m),
        S_OWN: (own, 0, block, to_s), S_Z: (zown, 0, block, to_s),
        S_A_LO: (xm, 0, block, to_s), S_A_HI: (xp, 0, block, to_s),
        S_B_LO: (zm, 0, block, to_s), S_B_HI: (zp, 0, block, to_s),
        S_RA: (xx, 0, block, to_s), S_RB: (zx, 0, block, to_s),
    }
    arrives = {
        Z: (zown, core, 0, block),
        A_LO: (xm, core, 0, block), A_HI: (xp, core, 0, block),
        B_LO: (zm, core, 0, block), B_HI: (zp, core, 0, block),
        RA_LO: (xx, core, 0, first), RA_HI: (xx, core, first, second),
        RB_LO: (zx, core, first, second), RB_HI: (zx, core, 0, first),
    }
    for kind in range(S_OWN, KINDS):
        arrives[kind] = (sends[kind][0], 1 - core, 0, block)

    def put(kind, t):
        c, lo, n, target = sends[kind]
        remote(kind, t, c, core, target, lo, n).start()

    def got(kind, t):
        c, k, lo, n = arrives[kind]
        remote(kind, t, c, k, to_s, lo, n).wait_recv()

    put(Z, 0)

    for c in small_loads[2:]:
        c.wait()
    rank_rows = pack(ag, au)
    for k in range(3):
        fac[k * SMALL:(k + 1) * SMALL, :] = rank_rows
    fac[3 * SMALL:, :] = jnp.zeros((LANES - 3 * SMALL, fac.shape[1]), BF16)
    fit = fit_ref[...].astype(F32)
    row16 = lax.broadcasted_iota(jnp.int32, (SMALL, LANES), 0)
    f0 = jnp.broadcast_to(fit[:, 0:1], (SMALL, LANES))
    f1 = jnp.broadcast_to(fit[:, 1:2], (SMALL, LANES))
    fit_rows = jnp.where(row16 // 4 % 2 == 0, f0, f1).astype(BF16)
    for q in range(n_pop):
        msg[q, :, :depth] = rank_rows[:, q * depth:(q + 1) * depth]
        msg[q, :, depth:] = fit_rows

    def factor_copy(q):
        return pltpu.make_async_remote_copy(
            src_ref=msg.at[q], dst_ref=abuf.at[sh], send_sem=asend.at[q], recv_sem=arecv.at[0],
            device_id=(q, sh), device_id_type=MESH,
        )

    def spread_copy(s, target):
        return pltpu.make_async_remote_copy(
            src_ref=abuf.at[s], dst_ref=abuf.at[s], send_sem=bsend.at[target], recv_sem=brecv.at[s],
            device_id=(pop, target), device_id_type=MESH,
        )

    @pl.when(pop == sh)
    def _():
        @pl.loop(1, n_pop)
        def _(d):
            factor_copy((pop + d) % n_pop).start()
        abuf[pop] = msg[pop]

    total[...] = jnp.zeros_like(total)

    def project():
        for c in tok_loads:
            c.wait()
        acc[0, :, :LANES] = jnp.zeros((rows, LANES), F32)

        @pl.loop(0, tok.shape[1] // span)
        def _(k):
            cols = pl.ds(pl.multiple_of(k * span, span), span)
            acc[0, :, :LANES] += dot(tok[:, cols], fac[:, cols], ((1,), (1,)))

        row = lax.broadcasted_iota(jnp.int32, (rows, LANES), 0)
        lane = lax.broadcasted_iota(jnp.int32, (rows, LANES), 1)
        mine = (row // per_member) == (lane // 4 % 2)
        p = jnp.where(mine, acc[0, :, :LANES] * noise, 0.0)
        hi = p.astype(BF16).astype(F32)
        mid = (p - hi).astype(BF16).astype(F32)
        lo = p - hi - mid
        group = lane // SMALL
        ext[...] = jnp.where(group == 0, hi, jnp.where(group == 1, mid, lo)).astype(BF16)

    def split_rows(v):
        n = v.shape[0]
        gate_row = lax.broadcasted_iota(jnp.int32, (n, LANES), 0) % SMALL < SMALL // 2
        vf = v.astype(F32)
        return jnp.concatenate(
            [jnp.where(gate_row, vf, 0.0), jnp.where(gate_row, 0.0, vf)], axis=1
        ).astype(BF16)

    def start_chunk(t, slot):
        rhs = split_rows(gath[t, own, core, 2 * depth:, :])
        pad = jnp.zeros((LANES - 3 * SMALL, 2 * LANES), BF16)
        acc[slot] = dot(ext[...], jnp.concatenate([rhs, rhs, rhs, pad], axis=0))

    def add_chip(t, slot, c):
        cols = pl.ds(pl.multiple_of(c * span, span), span)
        gate = gath[t, c, :, :depth, :].reshape(span, LANES)
        up = gath[t, c, :, depth:2 * depth, :].reshape(span, LANES)
        acc[slot] += dot(tok[:, cols], jnp.concatenate([gate, up], axis=1))

    def finish_chunk(t, slot):
        gate, up = acc[slot, :, :LANES], acc[slot, :, LANES:]
        hidden = gate / (1.0 + jnp.exp(-gate)) * up
        total[...] += hidden * ro_ref[pl.ds(t, 1), :]

    def build_left():
        a = abuf[:, :, :depth].reshape(n_pop * SMALL, depth).astype(F32)
        f = abuf[:, :, depth:].reshape(n_pop * SMALL, LANES).astype(F32)
        prod = (a * jnp.concatenate([f] * (depth // LANES), axis=1)).T
        hi = prod.astype(BF16)
        left[:, :n_pop * SMALL] = hi
        left[:, n_pop * SMALL:] = (prod - hi.astype(F32)).astype(BF16)

    def out_copy(t, k):
        dst = (ug_hbm, uu_hbm)[k]
        col = pl.multiple_of(t * LANES, LANES)
        return pltpu.make_async_copy(stage.at[t, k], dst.at[:, pl.ds(col, LANES)], osem.at[k, t])

    def update_chunk(t):
        right = split_rows(gath[t, :, :, 2 * depth:, :].reshape(n_pop * SMALL, LANES))
        upd = dot(left[...], jnp.concatenate([right, right], axis=0)) * out_scale
        stage[t, 0] = upd[:, :LANES]
        stage[t, 1] = upd[:, LANES:]
        out_copy(t, 0).start()
        out_copy(t, 1).start()

    def phase_two(t, slot):
        got(S_RA, t)
        add_chip(t, slot, xx)
        got(S_RB, t)
        add_chip(t, slot, zx)
        finish_chunk(t, slot)

    @pl.loop(0, chunks + 2)
    def _(i):
        @pl.when(i < chunks)
        def _():
            put(A_LO, i)
            put(A_HI, i)

            @pl.when(i + 1 < chunks)
            def _():
                put(Z, i + 1)
            put(S_OWN, i)
            got(Z, i)
            put(B_LO, i)
            put(B_HI, i)
            put(S_Z, i)

        @pl.when((i >= 1) & (i < chunks + 1))
        def _():
            t = i - 1
            for kind, relay, copy in (
                (A_LO, RA_LO, S_A_LO), (A_HI, RA_HI, S_A_HI),
                (B_LO, RB_LO, S_B_LO), (B_HI, RB_HI, S_B_HI),
            ):
                got(kind, t)
                put(relay, t)
                put(copy, t)

        @pl.when(i >= 2)
        def _():
            t = i - 2
            got(RA_LO, t)
            got(RA_HI, t)
            put(S_RA, t)
            got(RB_LO, t)
            got(RB_HI, t)
            put(S_RB, t)

        @pl.when(i == 0)
        def _():
            project()

        @pl.when(i == 1)
        def _():
            @pl.when(pop != sh)
            def _():
                factor_copy(pop).wait_recv()

            @pl.loop(1, n_shard)
            def _(d):
                spread_copy(sh, (sh + d) % n_shard).start()

        @pl.when((i >= 1) & (i < chunks + 1))
        def _():
            t = i - 1
            for kind in (S_OWN, S_Z, S_A_LO, S_A_HI, S_B_LO, S_B_HI):
                got(kind, t)
            start_chunk(t, t % 2)

            @pl.loop(0, 6)
            def _(j):
                q = j // 2
                add_chip(t, t % 2, at(q + q // 2, j % 2))

        @pl.when(i >= 2)
        def _():
            phase_two(i - 2, i % 2)

        @pl.when(i == 2)
        def _():
            @pl.loop(1, n_shard)
            def _(d):
                spread_copy((sh + d) % n_shard, sh).wait_recv()
            build_left()

        @pl.when((i >= 2) & (i < chunks + 1))
        def _():
            update_chunk(i - 2)

    ones = jnp.ones((8, LANES), F32)
    for m in range(members):
        part = dot(ones, total[m * per_member:(m + 1) * per_member, :], ((1,), (1,)), lax.Precision.HIGHEST)
        parts[sh, m:m + 1, :] = part[0:1, :]

    def score_copy(s, target):
        return pltpu.make_async_remote_copy(
            src_ref=parts.at[s], dst_ref=parts.at[s], send_sem=psend.at[target], recv_sem=precv.at[s],
            device_id=(pop, target), device_id_type=MESH,
        )

    @pl.loop(1, n_shard)
    def _(d):
        score_copy(sh, (sh + d) % n_shard).start()

    update_chunk(chunks - 1)

    @pl.loop(0, chunks)
    def _(t):
        for kind in range(KINDS):
            c, lo, n, target = sends[kind]
            remote(kind, t, c, core, target, lo, n).wait_send()

    @pl.when(pop == sh)
    def _():
        @pl.loop(1, n_pop)
        def _(d):
            factor_copy((pop + d) % n_pop).wait_send()

    @pl.loop(1, n_shard)
    def _(d):
        spread_copy(sh, (sh + d) % n_shard).wait_send()
        score_copy(sh, (sh + d) % n_shard).wait_send()

    @pl.loop(1, n_shard)
    def _(d):
        score_copy((sh + d) % n_shard, sh).wait_recv()

    score = parts[0]
    for s in range(1, n_shard):
        score = score + parts[s]
    sc_ref[...] = score

    @pl.loop(0, chunks)
    def _(t):
        out_copy(t, 0).wait()
        out_copy(t, 1).wait()


def body(n_pop, n_shard, tokens, wg, wu, a_gate, a_up, h_gate, h_up, fitness, readout):
    members, tok_count, width = tokens.shape
    depth, cols = wg.shape
    ranks = a_gate.shape[1]
    chunks = cols // LANES
    rows = members * tok_count
    chips = n_pop // CORES
    noise = 0.25 / math.sqrt(width * ranks)
    out_scale = 1.0 / math.sqrt(n_pop * members * ranks)
    block = 2 * depth + SMALL
    dma = pltpu.SemaphoreType.DMA
    anyspec = pl.BlockSpec(memory_space=pl.ANY)
    vspec = pl.BlockSpec(memory_space=pltpu.VMEM)
    return pl.pallas_call(
        functools.partial(kernel, noise, out_scale, n_pop, n_shard),
        name="generation",
        out_shape=(
            jax.ShapeDtypeStruct((members, tok_count), F32),
            jax.ShapeDtypeStruct((depth, cols), F32),
            jax.ShapeDtypeStruct((depth, cols), F32),
        ),
        in_specs=[anyspec] * 7 + [vspec, vspec],
        out_specs=(vspec, anyspec, anyspec),
        scratch_shapes=[
            pltpu.VMEM((rows, width), BF16),
            pltpu.VMEM((chunks, chips, CORES, block, LANES), BF16),
            pltpu.VMEM((2, rows, 2 * LANES), F32),
            pltpu.VMEM((rows, LANES), F32),
            pltpu.VMEM((rows, LANES), BF16),
            pltpu.VMEM((LANES, width), BF16),
            pltpu.VMEM((members, ranks, width), BF16),
            pltpu.VMEM((members, ranks, width), BF16),
            pltpu.VMEM((members, ranks, cols), BF16),
            pltpu.VMEM((members, ranks, cols), BF16),
            pltpu.VMEM((n_pop, SMALL, depth + LANES), BF16),
            pltpu.VMEM((n_pop, SMALL, depth + LANES), BF16),
            pltpu.VMEM((depth, 2 * n_pop * SMALL), BF16),
            pltpu.VMEM((chunks, 2, depth, LANES), F32),
            pltpu.VMEM((n_shard, members, tok_count), F32),
            dma((KINDS, chunks)), dma((KINDS, chunks)),
            dma((2, chunks)), dma((6,)),
            dma((n_pop,)), dma((1,)),
            dma((n_shard,)), dma((n_shard,)),
            dma((n_shard,)), dma((n_shard,)),
            dma((2, chunks)),
        ],
        compiler_params=pltpu.CompilerParams(
            collective_id=0, has_side_effects=True, vmem_limit_bytes=56 * 1024 * 1024
        ),
    )(tokens, wg, wu, a_gate, a_up, h_gate, h_up, fitness.reshape(1, members), readout.reshape(chunks, LANES))


def solution(mesh):
    placed = (
        P("pop", None, None),
        P("pop", "shard"),
        P("pop", "shard"),
        P("pop", None, None),
        P("pop", None, None),
        P("pop", None, "shard"),
        P("pop", None, "shard"),
        P("pop"),
        P("shard"),
    )
    return jax.shard_map(
        functools.partial(body, mesh.shape["pop"], mesh.shape["shard"]),
        mesh=mesh,
        in_specs=placed,
        out_specs=(P("pop", None), P("pop", "shard"), P("pop", "shard")),
        check_vma=False,
    )
```

```python
import functools
import math

import jax
import jax.numpy as jnp
from jax import lax
from jax.experimental import pallas as pl
from jax.experimental.pallas import tpu as pltpu
from jax.sharding import PartitionSpec as P

MESH = pl.DeviceIdType.MESH
F32 = jnp.float32
BF16 = jnp.bfloat16
LANES = 128
RING = 4
CORES = 2
SMALL = 16
(Z, ZX, A_LO, A_HI, B_LO, B_HI, RA_LO, RA_HI, RB_LO, RB_HI,
 S_OWN, S_Z, S_A_LO, S_A_HI, S_B_LO, S_B_HI, S_RA, S_RB) = range(18)
KINDS = 18


def dot(a, b, dims=((1,), (0,)), precision=None):
    return lax.dot_general(a, b, (dims, ((), ())), precision=precision, preferred_element_type=F32)


def split_rows(v):
    n = v.shape[0]
    gate_row = lax.broadcasted_iota(jnp.int32, (n, LANES), 0) % SMALL < SMALL // 2
    vf = v.astype(F32)
    return jnp.concatenate(
        [jnp.where(gate_row, vf, 0.0), jnp.where(gate_row, 0.0, vf)], axis=1
    ).astype(BF16)


def kernel(
    noise, n_pop, n_shard,
    tok_hbm, wg_hbm, wu_hbm, ag_hbm, au_hbm, hg_hbm, hu_hbm, fit_hbm, ro_hbm,
    sc_ref, left, right_hbm,
    tok, gath, acc, total, ext, fac, ag, au, hg, hu, fit_ref, ro_ref, msg, abuf, parts,
    send, recv, wsem, lsem, asend, arecv, bsend, brecv, psend, precv, osem,
):
    pop, sh = lax.axis_index("pop"), lax.axis_index("shard")
    core, chip = pop % CORES, pop // CORES
    x, zh = chip % RING, chip // RING
    chunks = gath.shape[0]
    depth = wg_hbm.shape[0]
    rows = tok.shape[0]
    members = tok_hbm.shape[0]
    per_member = rows // members
    block = 2 * depth + SMALL
    first = depth + SMALL
    span = CORES * depth

    def at(dx, dz):
        return (zh + dz) % 2 * RING + (x + dx) % RING

    def dev(c, k):
        return (c * CORES + k, sh)

    own, zown = at(0, 0), at(0, 1)
    xp, xm, xx = at(1, 0), at(3, 0), at(2, 0)
    zp, zm, zx = at(1, 1), at(3, 1), at(2, 1)

    def weight_load(t, k):
        src = (wg_hbm, wu_hbm)[k]
        col = pl.multiple_of(t * LANES, LANES)
        return pltpu.make_async_copy(
            src.at[:, pl.ds(col, LANES)], gath.at[t, own, core, pl.ds(k * depth, depth)], wsem.at[k, t]
        )

    small_loads = [
        pltpu.make_async_copy(a, b, lsem.at[i])
        for i, (a, b) in enumerate(((hg_hbm, hg), (hu_hbm, hu), (ag_hbm, ag), (au_hbm, au), (fit_hbm, fit_ref), (ro_hbm, ro_ref)))
    ]
    tok_loads = [
        pltpu.make_async_copy(
            tok_hbm.at[m], tok.at[pl.ds(m * per_member, per_member)], lsem.at[6 + m]
        )
        for m in range(members)
    ]
    for c in small_loads[:2]:
        c.start()

    @pl.loop(0, chunks)
    def _(t):
        weight_load(t, 0).start()
        weight_load(t, 1).start()

    for c in small_loads[2:] + tok_loads:
        c.start()

    barrier = pltpu.get_barrier_semaphore()

    @pl.loop(1, n_pop)
    def _(d):
        pl.semaphore_signal(barrier, inc=1, device_id=((pop + d) % n_pop, sh), device_id_type=MESH)

    @pl.loop(1, n_shard)
    def _(d):
        pl.semaphore_signal(barrier, inc=1, device_id=(pop, (sh + d) % n_shard), device_id_type=MESH)

    for c in small_loads[:2]:
        c.wait()

    def pack(gate, up):
        return jnp.concatenate(
            [gate[0].astype(F32), gate[1].astype(F32), up[0].astype(F32), up[1].astype(F32)], axis=0
        ).astype(BF16)

    factors = pack(hg, hu)
    for t in range(chunks):
        gath[t, own, core, 2 * depth:, :] = factors[:, t * LANES:(t + 1) * LANES]

    pl.semaphore_wait(barrier, n_pop - 1 + n_shard - 1)

    def remote(kind, t, c, k, target, lo=0, n=block):
        ref = gath.at[t, c, k, pl.ds(lo, n)]
        return pltpu.make_async_remote_copy(
            src_ref=ref, dst_ref=ref, send_sem=send.at[kind, t], recv_sem=recv.at[kind, t],
            device_id=target, device_id_type=MESH,
        )

    to_z, to_p, to_m, to_s = dev(zown, core), dev(xp, core), dev(xm, core), dev(own, 1 - core)
    second = block - first

    sends = {
        Z: (own, 0, block, to_z), ZX: (xx, 0, block, to_z),
        A_LO: (own, 0, block, to_p), A_HI: (own, 0, block, to_m),
        B_LO: (zown, 0, block, to_p), B_HI: (zown, 0, block, to_m),
        RA_LO: (xm, 0, first, to_p), RA_HI: (xp, first, second, to_m),
        RB_LO: (zm, first, second, to_p), RB_HI: (zp, 0, first, to_m),
        S_OWN: (own, 0, block, to_s), S_Z: (zown, 0, block, to_s),
        S_A_LO: (xm, 0, block, to_s), S_A_HI: (xp, 0, block, to_s),
        S_B_LO: (zm, 0, block, to_s), S_B_HI: (zp, 0, block, to_s),
        S_RA: (xx, 0, block, to_s), S_RB: (zx, 0, block, to_s),
    }
    arrives = {
        Z: (zown, core, 0, block), ZX: (zx, core, 0, block),
        A_LO: (xm, core, 0, block), A_HI: (xp, core, 0, block),
        B_LO: (zm, core, 0, block), B_HI: (zp, core, 0, block),
        RA_LO: (xx, core, 0, first), RA_HI: (xx, core, first, second),
        RB_LO: (zx, core, first, second), RB_HI: (zx, core, 0, first),
    }
    for kind in range(S_OWN, KINDS):
        arrives[kind] = (sends[kind][0], 1 - core, 0, block)

    def put(kind, t):
        c, lo, n, target = sends[kind]
        remote(kind, t, c, core, target, lo, n).start()

    def got(kind, t):
        c, k, lo, n = arrives[kind]
        remote(kind, t, c, k, to_s, lo, n).wait_recv()

    def open_chunk(t):
        weight_load(t, 0).wait()
        weight_load(t, 1).wait()
        for kind in (A_LO, A_HI, S_OWN):
            put(kind, t)

    def pass_a(t):
        for kind, relay, copy in ((A_LO, RA_LO, S_A_LO), (A_HI, RA_HI, S_A_HI)):
            got(kind, t)
            put(relay, t)
            put(copy, t)

    def over_z(t):
        return t == 3

    def far_sends(t, fn):
        @pl.when(over_z(t))
        def _():
            fn(ZX, t)

        @pl.when(jnp.logical_not(over_z(t)))
        def _():
            fn(RB_LO, t)
            fn(RB_HI, t)

    open_chunk(0)
    put(Z, 0)
    open_chunk(1)

    for c in small_loads[2:]:
        c.wait()
    rank_rows = pack(ag, au)
    for k in range(3):
        fac[k * SMALL:(k + 1) * SMALL, :] = rank_rows
    fac[3 * SMALL:, :] = jnp.zeros((LANES - 3 * SMALL, fac.shape[1]), BF16)
    fit = fit_ref[...].astype(F32)
    row16 = lax.broadcasted_iota(jnp.int32, (SMALL, LANES), 0)
    f0 = jnp.broadcast_to(fit[:, 0:1], (SMALL, LANES))
    f1 = jnp.broadcast_to(fit[:, 1:2], (SMALL, LANES))
    fit_rows = jnp.where(row16 // 4 % 2 == 0, f0, f1).astype(BF16)
    for q in range(n_pop):
        msg[q, :, :depth] = rank_rows[:, q * depth:(q + 1) * depth]
        msg[q, :, depth:] = fit_rows

    def factor_copy(q):
        return pltpu.make_async_remote_copy(
            src_ref=msg.at[q], dst_ref=abuf.at[sh], send_sem=asend.at[q], recv_sem=arecv.at[0],
            device_id=(q, sh), device_id_type=MESH,
        )

    def spread_copy(s, target):
        return pltpu.make_async_remote_copy(
            src_ref=abuf.at[s], dst_ref=abuf.at[s], send_sem=bsend.at[target], recv_sem=brecv.at[s],
            device_id=(pop, target), device_id_type=MESH,
        )

    @pl.when(pop == sh)
    def _():
        @pl.loop(1, n_pop)
        def _(d):
            factor_copy((pop + d) % n_pop).start()
        abuf[pop] = msg[pop]

    total[...] = jnp.zeros_like(total)

    def project():
        for c in tok_loads:
            c.wait()
        acc[0, :, :LANES] = jnp.zeros((rows, LANES), F32)

        @pl.loop(0, tok.shape[1] // span)
        def _(k):
            cols = pl.ds(pl.multiple_of(k * span, span), span)
            acc[0, :, :LANES] += dot(tok[:, cols], fac[:, cols], ((1,), (1,)))

        row = lax.broadcasted_iota(jnp.int32, (rows, LANES), 0)
        lane = lax.broadcasted_iota(jnp.int32, (rows, LANES), 1)
        mine = (row // per_member) == (lane // 4 % 2)
        p = jnp.where(mine, acc[0, :, :LANES] * noise, 0.0)
        hi = p.astype(BF16).astype(F32)
        mid = (p - hi).astype(BF16).astype(F32)
        lo = p - hi - mid
        group = lane // SMALL
        ext[...] = jnp.where(group == 0, hi, jnp.where(group == 1, mid, lo)).astype(BF16)

    def start_chunk(t, slot):
        rhs = split_rows(gath[t, own, core, 2 * depth:, :])
        pad = jnp.zeros((LANES - 3 * SMALL, 2 * LANES), BF16)
        acc[slot] = dot(ext[...], jnp.concatenate([rhs, rhs, rhs, pad], axis=0))

    def add_chip(t, slot, c):
        cols = pl.ds(pl.multiple_of(c * span, span), span)
        gate = gath[t, c, :, :depth, :].reshape(span, LANES)
        up = gath[t, c, :, depth:2 * depth, :].reshape(span, LANES)
        acc[slot] += dot(tok[:, cols], jnp.concatenate([gate, up], axis=1))

    def finish_chunk(t, slot):
        gate, up = acc[slot, :, :LANES], acc[slot, :, LANES:]
        hidden = gate / (1.0 + jnp.exp(-gate)) * up
        total[...] += hidden * ro_ref[pl.ds(t, 1), :]

    def build_left():
        a = abuf[:, :, :depth].reshape(n_pop * SMALL, depth).astype(F32)
        f = abuf[:, :, depth:].reshape(n_pop * SMALL, LANES).astype(F32)
        prod = (a * jnp.concatenate([f] * (depth // LANES), axis=1)).T
        hi = prod.astype(BF16)
        left[:, :n_pop * SMALL] = hi
        left[:, n_pop * SMALL:] = (prod - hi.astype(F32)).astype(BF16)

    def factor_out(t):
        return pltpu.make_async_copy(gath.at[t, :, :, pl.ds(2 * depth, SMALL)], right_hbm.at[t], osem.at[t])

    open_chunk(2)
    put(Z, 1)
    pass_a(0)

    @pl.loop(0, chunks + 2)
    def _(i):
        @pl.when(i + 3 < chunks)
        def _():
            open_chunk(i + 3)

        @pl.when(i + 1 < chunks)
        def _():
            pass_a(i + 1)

        @pl.when(i < chunks)
        def _():
            got(Z, i)
            for kind in (B_LO, B_HI):
                put(kind, i)

            @pl.when(i + 2 < chunks)
            def _():
                put(Z, i + 2)
            put(S_Z, i)

        @pl.when((i >= 1) & (i < chunks + 1))
        def _():
            t = i - 1
            for kind in (S_OWN, S_Z, S_A_LO, S_A_HI, S_RA):
                got(kind, t)
            start_chunk(t, t % 2)

            add_chip(t, t % 2, zown)

            @pl.loop(0, RING)
            def _(j):
                add_chip(t, t % 2, at(j, 0))

        @pl.when((i >= 1) & (i < chunks + 1))
        def _():
            t = i - 1
            for kind, relay, copy in ((B_LO, RB_LO, S_B_LO), (B_HI, RB_HI, S_B_HI)):
                got(kind, t)

                @pl.when(jnp.logical_not(over_z(t)))
                def _():
                    put(relay, t)
                put(copy, t)

        @pl.when(i < chunks)
        def _():
            got(RA_LO, i)
            got(RA_HI, i)

            @pl.when(over_z(i))
            def _():
                put(ZX, i)
            put(S_RA, i)

        @pl.when(i >= 2)
        def _():
            far_sends(i - 2, got)
            put(S_RB, i - 2)

        @pl.when(i == 0)
        def _():
            project()

        @pl.when(i == 1)
        def _():
            @pl.when(pop != sh)
            def _():
                factor_copy(pop).wait_recv()

            @pl.loop(1, n_shard)
            def _(d):
                spread_copy(sh, (sh + d) % n_shard).start()

        @pl.when((i >= 1) & (i < chunks + 1))
        def _():
            t = i - 1
            got(S_B_LO, t)
            got(S_B_HI, t)

            @pl.loop(0, 2)
            def _(j):
                add_chip(t, t % 2, at(1 + 2 * j, 1))

        @pl.when(i >= 2)
        def _():
            got(S_RB, i - 2)
            add_chip(i - 2, i % 2, zx)
            finish_chunk(i - 2, i % 2)
            factor_out(i - 2).start()

        @pl.when(i == chunks - 1)
        def _():
            @pl.loop(1, n_shard)
            def _(d):
                spread_copy((sh + d) % n_shard, sh).wait_recv()
            build_left()

    ones = jnp.ones((8, LANES), F32)
    for m in range(members):
        part = dot(ones, total[m * per_member:(m + 1) * per_member, :], ((1,), (1,)), lax.Precision.HIGHEST)
        parts[sh, m:m + 1, :] = part[0:1, :]

    def score_copy(s, target):
        return pltpu.make_async_remote_copy(
            src_ref=parts.at[s], dst_ref=parts.at[s], send_sem=psend.at[target], recv_sem=precv.at[s],
            device_id=(pop, target), device_id_type=MESH,
        )

    @pl.loop(1, n_shard)
    def _(d):
        score_copy(sh, (sh + d) % n_shard).start()

    def sent(kind, t):
        c, lo, n, target = sends[kind]
        remote(kind, t, c, core, target, lo, n).wait_send()

    @pl.loop(0, chunks)
    def _(t):
        for kind in range(KINDS):
            if kind not in (ZX, RB_LO, RB_HI):
                sent(kind, t)
        far_sends(t, sent)

    @pl.when(pop == sh)
    def _():
        @pl.loop(1, n_pop)
        def _(d):
            factor_copy((pop + d) % n_pop).wait_send()

    @pl.loop(1, n_shard)
    def _(d):
        spread_copy(sh, (sh + d) % n_shard).wait_send()
        score_copy(sh, (sh + d) % n_shard).wait_send()

    @pl.loop(1, n_shard)
    def _(d):
        score_copy((sh + d) % n_shard, sh).wait_recv()

    score = parts[0]
    for s in range(1, n_shard):
        score = score + parts[s]
    sc_ref[...] = score

    @pl.loop(0, chunks)
    def _(t):
        factor_out(t).wait()


def finish_kernel(out_scale, score_ref, left, right, sc_ref, ug_ref, uu_ref):
    sc_ref[...] = score_ref[...]
    for t in range(right.shape[0]):
        rows = split_rows(right[t].reshape(left.shape[1] // 2, LANES))
        upd = dot(left[...], jnp.concatenate([rows, rows], axis=0)) * out_scale
        ug_ref[:, t * LANES:(t + 1) * LANES] = upd[:, :LANES]
        uu_ref[:, t * LANES:(t + 1) * LANES] = upd[:, LANES:]


def body(n_pop, n_shard, tokens, wg, wu, a_gate, a_up, h_gate, h_up, fitness, readout):
    members, tok_count, width = tokens.shape
    depth, cols = wg.shape
    ranks = a_gate.shape[1]
    chunks = cols // LANES
    rows = members * tok_count
    chips = n_pop // CORES
    noise = 0.25 / math.sqrt(width * ranks)
    out_scale = 1.0 / math.sqrt(n_pop * members * ranks)
    block = 2 * depth + SMALL
    dma = pltpu.SemaphoreType.DMA
    anyspec = pl.BlockSpec(memory_space=pl.ANY)
    vspec = pl.BlockSpec(memory_space=pltpu.VMEM)
    score, left, right = pl.pallas_call(
        functools.partial(kernel, noise, n_pop, n_shard),
        name="generation",
        out_shape=(
            jax.ShapeDtypeStruct((members, tok_count), F32),
            jax.ShapeDtypeStruct((depth, 2 * n_pop * SMALL), BF16),
            jax.ShapeDtypeStruct((chunks, chips, CORES, SMALL, LANES), BF16),
        ),
        in_specs=[anyspec] * 9,
        out_specs=(vspec, vspec, anyspec),
        scratch_shapes=[
            pltpu.VMEM((rows, width), BF16),
            pltpu.VMEM((chunks, chips, CORES, block, LANES), BF16),
            pltpu.VMEM((2, rows, 2 * LANES), F32),
            pltpu.VMEM((rows, LANES), F32),
            pltpu.VMEM((rows, LANES), BF16),
            pltpu.VMEM((LANES, width), BF16),
            pltpu.VMEM((members, ranks, width), BF16),
            pltpu.VMEM((members, ranks, width), BF16),
            pltpu.VMEM((members, ranks, cols), BF16),
            pltpu.VMEM((members, ranks, cols), BF16),
            pltpu.VMEM((1, members), BF16),
            pltpu.VMEM((chunks, LANES), F32),
            pltpu.VMEM((n_pop, SMALL, depth + LANES), BF16),
            pltpu.VMEM((n_pop, SMALL, depth + LANES), BF16),
            pltpu.VMEM((n_shard, members, tok_count), F32),
            dma((KINDS, chunks)), dma((KINDS, chunks)),
            dma((2, chunks)), dma((8,)),
            dma((n_pop,)), dma((1,)),
            dma((n_shard,)), dma((n_shard,)),
            dma((n_shard,)), dma((n_shard,)),
            dma((chunks,)),
        ],
        compiler_params=pltpu.CompilerParams(
            collective_id=0, has_side_effects=True, vmem_limit_bytes=56 * 1024 * 1024
        ),
    )(tokens, wg, wu, a_gate, a_up, h_gate, h_up, fitness.reshape(1, members), readout.reshape(chunks, LANES))
    return pl.pallas_call(
        functools.partial(finish_kernel, out_scale),
        name="updates",
        out_shape=(
            jax.ShapeDtypeStruct((members, tok_count), F32),
            jax.ShapeDtypeStruct((depth, cols), F32),
            jax.ShapeDtypeStruct((depth, cols), F32),
        ),
        in_specs=[vspec] * 3,
        out_specs=(vspec,) * 3,
    )(score, left, right)


def solution(mesh):
    placed = (
        P("pop", None, None),
        P("pop", "shard"),
        P("pop", "shard"),
        P("pop", None, None),
        P("pop", None, None),
        P("pop", None, "shard"),
        P("pop", None, "shard"),
        P("pop"),
        P("shard"),
    )
    return jax.shard_map(
        functools.partial(body, mesh.shape["pop"], mesh.shape["shard"]),
        mesh=mesh,
        in_specs=placed,
        out_specs=(P("pop", None), P("pop", "shard"), P("pop", "shard")),
        check_vma=False,
    )
```

```python
import functools
import math

import jax
import jax.numpy as jnp
from jax import lax
from jax.experimental import pallas as pl
from jax.experimental.pallas import tpu as pltpu
from jax.sharding import PartitionSpec as P

MESH = pl.DeviceIdType.MESH
F32 = jnp.float32
BF16 = jnp.bfloat16
LANES = 128
RING = 4
CORES = 2
SMALL = 16
(Z, A_LO, A_HI, B_LO, B_HI, RA_LO, RA_HI, RB_LO, RB_HI,
 S_OWN, S_Z, S_A_LO, S_A_HI, S_B_LO, S_B_HI, S_RA, S_RB) = range(17)
BLOCKS = 15
W_Z, W_A_LO, W_A_HI, W_B_LO, W_B_HI, W_RA, W_RB, W_S_FIRST, W_S_B, W_S_RB = range(10)
WAITS = 10
BRINGS = {W_S_FIRST: 5, W_S_B: 2}
LANDS = {
    Z: W_Z, A_LO: W_A_LO, A_HI: W_A_HI, B_LO: W_B_LO, B_HI: W_B_HI,
    RA_LO: W_RA, RA_HI: W_RA, RB_LO: W_RB, RB_HI: W_RB,
    S_OWN: W_S_FIRST, S_Z: W_S_FIRST, S_A_LO: W_S_FIRST, S_A_HI: W_S_FIRST, S_RA: W_S_FIRST,
    S_B_LO: W_S_B, S_B_HI: W_S_B, S_RB: W_S_RB,
}


def dot(a, b, dims=((1,), (0,)), precision=None):
    return lax.dot_general(a, b, (dims, ((), ())), precision=precision, preferred_element_type=F32)


def three_terms(v):
    hi = v.astype(BF16)
    rest = v - hi.astype(F32)
    mid = rest.astype(BF16)
    return hi, mid, (rest - mid.astype(F32)).astype(BF16)


def by_kind(v, n):
    v = v.astype(F32).reshape(n, SMALL, v.shape[-1])
    half = SMALL // 2
    return [v[:, k * half:(k + 1) * half].reshape(n * half, v.shape[-1]) for k in range(2)]


def split_rows(v):
    n = v.shape[0]
    gate_row = lax.broadcasted_iota(jnp.int32, (n, LANES), 0) % SMALL < SMALL // 2
    vf = v.astype(F32)
    return jnp.concatenate(
        [jnp.where(gate_row, vf, 0.0), jnp.where(gate_row, 0.0, vf)], axis=1
    ).astype(BF16)


def kernel(
    noise, n_pop, n_shard,
    tok_hbm, wg_hbm, wu_hbm, ag_hbm, au_hbm, hg_hbm, hu_hbm, fit_hbm, ro_hbm,
    sc_ref, left_hbm, right_hbm,
    tok, gath, acc, total, ext, fac, ag, au, hg, hu, fit_ref, ro_ref, msg, abuf, left, parts,
    send, recv, wsem, lsem, asend, arecv, bsend, brecv, psend, precv, osem,
):
    pop, sh = lax.axis_index("pop"), lax.axis_index("shard")
    core, chip = pop % CORES, pop // CORES
    x, zh = chip % RING, chip // RING
    chunks = recv.shape[1]
    chips = n_pop // CORES
    depth = wg_hbm.shape[0]
    rows = tok.shape[0]
    members = tok_hbm.shape[0]
    per_member = rows // members
    block = 2 * depth + SMALL
    first = depth + SMALL
    span = CORES * depth

    def at(dx, dz):
        return (zh + dz) % 2 * RING + (x + dx) % RING

    def place(t, c, k=0):
        return (t * chips + c) * CORES + k

    def dev(c, k):
        return (c * CORES + k, sh)

    own, zown = at(0, 0), at(0, 1)
    xp, xm, xx = at(1, 0), at(3, 0), at(2, 0)
    zp, zm, zx = at(1, 1), at(3, 1), at(2, 1)

    def weight_load(t, k):
        src = (wg_hbm, wu_hbm)[k]
        col = pl.multiple_of(t * LANES, LANES)
        return pltpu.make_async_copy(
            src.at[:, pl.ds(col, LANES)],
            gath.at[place(t, own, core), pl.ds(k * depth, depth)], wsem.at[t],
        )

    small_loads = [
        pltpu.make_async_copy(a, b, lsem.at[i])
        for i, (a, b) in enumerate(((hg_hbm, hg), (hu_hbm, hu), (ag_hbm, ag), (au_hbm, au), (fit_hbm, fit_ref), (ro_hbm, ro_ref)))
    ]
    tok_loads = [
        pltpu.make_async_copy(
            tok_hbm.at[m], tok.at[pl.ds(m * per_member, per_member)], lsem.at[6 + m]
        )
        for m in range(members)
    ]
    for c in small_loads[:2]:
        c.start()

    @pl.loop(0, chunks)
    def _(t):
        weight_load(t, 0).start()
        weight_load(t, 1).start()

    for c in small_loads[2:] + tok_loads:
        c.start()

    barrier = pltpu.get_barrier_semaphore()

    @pl.loop(1, n_pop)
    def _(d):
        pl.semaphore_signal(barrier, inc=1, device_id=((pop + d) % n_pop, sh), device_id_type=MESH)

    @pl.loop(1, n_shard)
    def _(d):
        pl.semaphore_signal(barrier, inc=1, device_id=(pop, (sh + d) % n_shard), device_id_type=MESH)

    for c in small_loads[:2]:
        c.wait()

    def pack(gate, up):
        return jnp.concatenate(
            [gate[0].astype(F32), gate[1].astype(F32), up[0].astype(F32), up[1].astype(F32)], axis=0
        ).astype(BF16)

    factors = pack(hg, hu)
    for t in range(chunks):
        gath[place(t, own, core), 2 * depth:, :] = factors[:, t * LANES:(t + 1) * LANES]

    pl.semaphore_wait(barrier, n_pop - 1 + n_shard - 1)

    def remote(kind, t, c, target, lo=0, n=block):
        ref = gath.at[place(t, c, core), pl.ds(lo, n)]
        return pltpu.make_async_remote_copy(
            src_ref=ref, dst_ref=ref, send_sem=send.at[0], recv_sem=recv.at[LANDS[kind], t],
            device_id=target, device_id_type=MESH,
        )

    to_z, to_p, to_m, to_s = dev(zown, core), dev(xp, core), dev(xm, core), dev(own, 1 - core)
    second = block - first

    sends = {
        Z: (own, 0, block, to_z),
        A_LO: (own, 0, block, to_p), A_HI: (own, 0, block, to_m),
        B_LO: (zown, 0, block, to_p), B_HI: (zown, 0, block, to_m),
        RA_LO: (xm, 0, first, to_p), RA_HI: (xp, first, second, to_m),
        RB_LO: (zm, first, second, to_p), RB_HI: (zp, 0, first, to_m),
        S_OWN: (own, 0, block, to_s), S_Z: (zown, 0, block, to_s),
        S_A_LO: (xm, 0, block, to_s), S_A_HI: (xp, 0, block, to_s),
        S_B_LO: (zm, 0, block, to_s), S_B_HI: (zp, 0, block, to_s),
        S_RA: (xx, 0, block, to_s), S_RB: (zx, 0, block, to_s),
    }
    def put(kind, t):
        c, lo, n, target = sends[kind]
        remote(kind, t, c, target, lo, n).start()

    def bulk(ref, send_sem, recv_sem):
        return pltpu.make_async_remote_copy(
            src_ref=ref, dst_ref=ref, send_sem=send_sem, recv_sem=recv_sem,
            device_id=to_s, device_id_type=MESH,
        )

    def got(what, t):
        bulk(gath.at[pl.ds(0, BRINGS.get(what, 1))], send.at[0], recv.at[what, t]).wait_recv()

    def open_chunk(t):
        both = gath.at[0, pl.ds(0, 2 * depth)]
        pltpu.make_async_copy(both, both, wsem.at[t]).wait()
        for kind in (A_LO, A_HI, S_OWN):
            put(kind, t)

    def pass_a(t):
        for what, relay, copy in ((W_A_LO, RA_LO, S_A_LO), (W_A_HI, RA_HI, S_A_HI)):
            got(what, t)
            put(relay, t)
            put(copy, t)

    open_chunk(0)
    put(Z, 0)
    open_chunk(1)

    for c in small_loads[2:]:
        c.wait()
    rank_rows = pack(ag, au)
    for k in range(3):
        fac[k * SMALL:(k + 1) * SMALL, :] = rank_rows
    fac[3 * SMALL:, :] = jnp.zeros((LANES - 3 * SMALL, fac.shape[1]), BF16)
    fit = fit_ref[...].astype(F32)
    row16 = lax.broadcasted_iota(jnp.int32, (SMALL, LANES), 0)
    f0 = jnp.broadcast_to(fit[:, 0:1], (SMALL, LANES))
    f1 = jnp.broadcast_to(fit[:, 1:2], (SMALL, LANES))
    fit_rows = jnp.where(row16 // 4 % 2 == 0, f0, f1).astype(BF16)
    for q in range(n_pop):
        msg[q, :, :depth] = rank_rows[:, q * depth:(q + 1) * depth]
        msg[q, :, depth:] = fit_rows

    def factor_copy(q):
        return pltpu.make_async_remote_copy(
            src_ref=msg.at[q], dst_ref=abuf.at[sh], send_sem=asend.at[0], recv_sem=arecv.at[0],
            device_id=(q, sh), device_id_type=MESH,
        )

    def spread_copy(target):
        return pltpu.make_async_remote_copy(
            src_ref=abuf.at[sh], dst_ref=abuf.at[sh], send_sem=bsend.at[0], recv_sem=brecv.at[0],
            device_id=(pop, target), device_id_type=MESH,
        )

    others = pl.ds(0, n_shard - 1)
    spread_all = bulk(abuf.at[others], bsend.at[0], brecv.at[0])

    @pl.when(pop == sh)
    def _():
        @pl.loop(1, n_pop)
        def _(d):
            factor_copy((pop + d) % n_pop).start()
        abuf[pop] = msg[pop]

    total[...] = jnp.zeros_like(total)

    def project():
        for c in tok_loads:
            c.wait()
        acc[0, :, :LANES] = jnp.zeros((rows, LANES), F32)

        @pl.loop(0, tok.shape[1] // span)
        def _(k):
            cols = pl.ds(pl.multiple_of(k * span, span), span)
            acc[0, :, :LANES] += dot(tok[:, cols], fac[:, cols], ((1,), (1,)))

        row = lax.broadcasted_iota(jnp.int32, (rows, LANES), 0)
        lane = lax.broadcasted_iota(jnp.int32, (rows, LANES), 1)
        mine = (row // per_member) == (lane // 4 % 2)
        p = jnp.where(mine, acc[0, :, :LANES] * noise, 0.0)
        hi, mid, lo = (v.astype(F32) for v in three_terms(p))
        group = lane // SMALL
        ext[...] = jnp.where(group == 0, hi, jnp.where(group == 1, mid, lo)).astype(BF16)

    def start_chunk(t, slot):
        rhs = split_rows(gath[place(t, own, core), 2 * depth:, :])
        pad = jnp.zeros((LANES - 3 * SMALL, 2 * LANES), BF16)
        acc[slot] = dot(ext[...], jnp.concatenate([rhs, rhs, rhs, pad], axis=0))

    def add_chip(t, slot, c):
        cols = pl.ds(pl.multiple_of(c * span, span), span)
        both = pl.ds(place(t, c), CORES)
        gate = gath[both, :depth, :].reshape(span, LANES)
        up = gath[both, depth:2 * depth, :].reshape(span, LANES)
        acc[slot] += dot(tok[:, cols], jnp.concatenate([gate, up], axis=1))

    def finish_chunk(t, slot):
        gate, up = acc[slot, :, :LANES], acc[slot, :, LANES:]
        hidden = gate / (1.0 + jnp.exp(-gate)) * up
        total[...] += hidden * ro_ref[pl.ds(t, 1), :]

    def build_left():
        a = abuf[:, :, :depth].reshape(n_pop * SMALL, depth).astype(F32)
        f = abuf[:, :, depth:].reshape(n_pop * SMALL, LANES).astype(F32)
        prod = a * jnp.concatenate([f] * (depth // LANES), axis=1)
        for k, part in enumerate(by_kind(prod, n_pop)):
            part = part.T
            hi = part.astype(BF16)
            n = part.shape[1]
            left[k, :, :n] = hi
            left[k, :, n:] = (part - hi.astype(F32)).astype(BF16)

    def left_out():
        return pltpu.make_async_copy(left, left_hbm, osem.at[1])

    def factor_out(t):
        return pltpu.make_async_copy(
            gath.at[pl.ds(place(t, 0), n_pop), pl.ds(2 * depth, SMALL)], right_hbm.at[t], osem.at[0]
        )

    open_chunk(2)
    put(Z, 1)
    pass_a(0)

    @pl.loop(0, chunks + 2)
    def _(i):
        @pl.when(i + 3 < chunks)
        def _():
            open_chunk(i + 3)

        @pl.when(i + 1 < chunks)
        def _():
            pass_a(i + 1)

        @pl.when(i < chunks)
        def _():
            got(W_Z, i)
            for kind in (B_LO, B_HI):
                put(kind, i)

            @pl.when(i + 2 < chunks)
            def _():
                put(Z, i + 2)
            put(S_Z, i)

        @pl.when((i >= 1) & (i < chunks + 1))
        def _():
            t = i - 1
            for what, relay, copy in ((W_B_LO, RB_LO, S_B_LO), (W_B_HI, RB_HI, S_B_HI)):
                got(what, t)
                put(relay, t)
                put(copy, t)

        @pl.when((i >= 1) & (i < chunks + 1))
        def _():
            t = i - 1
            got(W_S_FIRST, t)
            start_chunk(t, t % 2)

            add_chip(t, t % 2, zown)

            @pl.loop(0, RING)
            def _(j):
                add_chip(t, t % 2, at(j, 0))

        @pl.when(i < chunks)
        def _():
            got(W_RA, i)
            put(S_RA, i)

        @pl.when(i >= 2)
        def _():
            got(W_RB, i - 2)
            put(S_RB, i - 2)

        @pl.when(i == 0)
        def _():
            project()

        @pl.when(i == 1)
        def _():
            @pl.when(pop != sh)
            def _():
                factor_copy(pop).wait_recv()

            @pl.loop(1, n_shard)
            def _(d):
                spread_copy((sh + d) % n_shard).start()

        @pl.when((i >= 1) & (i < chunks + 1))
        def _():
            t = i - 1
            got(W_S_B, t)

            @pl.loop(0, 2)
            def _(j):
                add_chip(t, t % 2, at(1 + 2 * j, 1))

        @pl.when(i >= 2)
        def _():
            got(W_S_RB, i - 2)
            add_chip(i - 2, i % 2, zx)
            finish_chunk(i - 2, i % 2)
            factor_out(i - 2).start()

        @pl.when(i == chunks - 1)
        def _():
            spread_all.wait_recv()
            build_left()
            left_out().start()

    ones = jnp.ones((SMALL, 3 * LANES), BF16)
    for m in range(members):
        part = dot(ones, jnp.concatenate(three_terms(total[m * per_member:(m + 1) * per_member, :]), axis=1), ((1,), (1,)))
        parts[sh, m:m + 1, :] = part[0:1, :]

    def score_copy(target):
        return pltpu.make_async_remote_copy(
            src_ref=parts.at[sh], dst_ref=parts.at[sh], send_sem=psend.at[0], recv_sem=precv.at[0],
            device_id=(pop, target), device_id_type=MESH,
        )

    @pl.loop(1, n_shard)
    def _(d):
        score_copy((sh + d) % n_shard).start()

    bulk(gath.at[pl.ds(0, chunks * BLOCKS)], send.at[0], recv.at[0, 0]).wait_send()

    @pl.when(pop == sh)
    def _():
        bulk(msg.at[others], asend.at[0], arecv.at[0]).wait_send()

    spread_all.wait_send()
    pltpu.make_async_copy(right_hbm, right_hbm, osem.at[0]).wait()
    left_out().wait()
    score_all = bulk(parts.at[others], psend.at[0], precv.at[0])
    score_all.wait_send()
    score_all.wait_recv()

    score = parts[0]
    for s in range(1, n_shard):
        score = score + parts[s]
    sc_ref[...] = score


def finish_kernel(out_scale, score_ref, left, right, sc_ref, ug_ref, uu_ref):
    sc_ref[...] = score_ref[...]
    chunks, n = right.shape[0], left.shape[2] // SMALL
    for t in range(0, chunks, 2):
        pair = [by_kind(right[u].reshape(n * SMALL, LANES), n) for u in range(t, min(t + 2, chunks))]
        for k, out in enumerate((ug_ref, uu_ref)):
            rows = jnp.concatenate([p[k].astype(BF16) for p in pair], axis=1)
            out[:, t * LANES:t * LANES + rows.shape[1]] = (
                dot(left[k], jnp.concatenate([rows, rows], axis=0)) * out_scale
            )


def body(n_pop, n_shard, tokens, wg, wu, a_gate, a_up, h_gate, h_up, fitness, readout):
    members, tok_count, width = tokens.shape
    depth, cols = wg.shape
    ranks = a_gate.shape[1]
    chunks = cols // LANES
    rows = members * tok_count
    noise = 0.25 / math.sqrt(width * ranks)
    out_scale = 1.0 / math.sqrt(n_pop * members * ranks)
    block = 2 * depth + SMALL
    dma = pltpu.SemaphoreType.DMA
    anyspec = pl.BlockSpec(memory_space=pl.ANY)
    vspec = pl.BlockSpec(memory_space=pltpu.VMEM)
    score, left, right = pl.pallas_call(
        functools.partial(kernel, noise, n_pop, n_shard),
        name="generation",
        out_shape=(
            jax.ShapeDtypeStruct((members, tok_count), F32),
            jax.ShapeDtypeStruct((2, depth, n_pop * SMALL), BF16),
            jax.ShapeDtypeStruct((chunks, n_pop, SMALL, LANES), BF16),
        ),
        in_specs=[anyspec] * 9,
        out_specs=(vspec, anyspec, anyspec),
        scratch_shapes=[
            pltpu.VMEM((rows, width), BF16),
            pltpu.VMEM((chunks * n_pop, block, LANES), BF16),
            pltpu.VMEM((2, rows, 2 * LANES), F32),
            pltpu.VMEM((rows, LANES), F32),
            pltpu.VMEM((rows, LANES), BF16),
            pltpu.VMEM((LANES, width), BF16),
            pltpu.VMEM((members, ranks, width), BF16),
            pltpu.VMEM((members, ranks, width), BF16),
            pltpu.VMEM((members, ranks, cols), BF16),
            pltpu.VMEM((members, ranks, cols), BF16),
            pltpu.VMEM((1, members), BF16),
            pltpu.VMEM((chunks, LANES), F32),
            pltpu.VMEM((n_pop, SMALL, depth + LANES), BF16),
            pltpu.VMEM((n_pop, SMALL, depth + LANES), BF16),
            pltpu.VMEM((2, depth, n_pop * SMALL), BF16),
            pltpu.VMEM((n_shard, members, tok_count), F32),
            dma((1,)), dma((WAITS, chunks)),
            dma((chunks,)), dma((8,)),
            dma((1,)), dma((1,)), dma((1,)), dma((1,)), dma((1,)), dma((1,)),
            dma((2,)),
        ],
        compiler_params=pltpu.CompilerParams(
            collective_id=0, has_side_effects=True, vmem_limit_bytes=56 * 1024 * 1024
        ),
    )(tokens, wg, wu, a_gate, a_up, h_gate, h_up, fitness.reshape(1, members), readout.reshape(chunks, LANES))
    return pl.pallas_call(
        functools.partial(finish_kernel, out_scale),
        name="updates",
        out_shape=(
            jax.ShapeDtypeStruct((members, tok_count), F32),
            jax.ShapeDtypeStruct((depth, cols), F32),
            jax.ShapeDtypeStruct((depth, cols), F32),
        ),
        grid=(2,),
        in_specs=[
            pl.BlockSpec((members, tok_count), lambda i: (0, 0)),
            pl.BlockSpec((2, depth // 2, n_pop * SMALL), lambda i: (0, i, 0)),
            pl.BlockSpec((chunks, n_pop, SMALL, LANES), lambda i: (0, 0, 0, 0)),
        ],
        out_specs=(
            pl.BlockSpec((members, tok_count), lambda i: (0, 0)),
            pl.BlockSpec((depth // 2, cols), lambda i: (i, 0)),
            pl.BlockSpec((depth // 2, cols), lambda i: (i, 0)),
        ),
    )(score, left, right)


def solution(mesh):
    placed = (
        P("pop", None, None),
        P("pop", "shard"),
        P("pop", "shard"),
        P("pop", None, None),
        P("pop", None, None),
        P("pop", None, "shard"),
        P("pop", None, "shard"),
        P("pop"),
        P("shard"),
    )
    return jax.shard_map(
        functools.partial(body, mesh.shape["pop"], mesh.shape["shard"]),
        mesh=mesh,
        in_specs=placed,
        out_specs=(P("pop", None), P("pop", "shard"), P("pop", "shard")),
        check_vma=False,
    )
```

```python
import functools
import math

import jax
import jax.numpy as jnp
from jax import lax
from jax.experimental import pallas as pl
from jax.experimental.pallas import tpu as pltpu
from jax.sharding import PartitionSpec as P

MESH = pl.DeviceIdType.MESH
F32 = jnp.float32
BF16 = jnp.bfloat16
LANES = 128
RING = 4
CORES = 2
SMALL = 16
(Z, A_LO, A_HI, B_LO, B_HI, RA_LO, RA_HI, RB_LO, RB_HI,
 S_OWN, S_Z, S_A_LO, S_A_HI, S_B_LO, S_B_HI, S_RA, S_RB) = range(17)
BLOCKS = 15
W_Z, W_A_LO, W_A_HI, W_B_LO, W_B_HI, W_RA, W_RB, W_S_FIRST, W_S_B, W_S_RB = range(10)
WAITS = 10
BRINGS = {W_S_FIRST: 5, W_S_B: 2}
LANDS = {
    Z: W_Z, A_LO: W_A_LO, A_HI: W_A_HI, B_LO: W_B_LO, B_HI: W_B_HI,
    RA_LO: W_RA, RA_HI: W_RA, RB_LO: W_RB, RB_HI: W_RB,
    S_OWN: W_S_FIRST, S_Z: W_S_FIRST, S_A_LO: W_S_FIRST, S_A_HI: W_S_FIRST, S_RA: W_S_FIRST,
    S_B_LO: W_S_B, S_B_HI: W_S_B, S_RB: W_S_RB,
}


def dot(a, b, dims=((1,), (0,)), precision=None):
    return lax.dot_general(a, b, (dims, ((), ())), precision=precision, preferred_element_type=F32)


def three_terms(v):
    hi = v.astype(BF16)
    rest = v - hi.astype(F32)
    mid = rest.astype(BF16)
    return hi, mid, (rest - mid.astype(F32)).astype(BF16)


def by_kind(v, n):
    v = v.astype(F32).reshape(n, SMALL, v.shape[-1])
    half = SMALL // 2
    return [v[:, k * half:(k + 1) * half].reshape(n * half, v.shape[-1]) for k in range(2)]


def split_rows(v):
    n = v.shape[0]
    gate_row = lax.broadcasted_iota(jnp.int32, (n, LANES), 0) % SMALL < SMALL // 2
    vf = v.astype(F32)
    return jnp.concatenate(
        [jnp.where(gate_row, vf, 0.0), jnp.where(gate_row, 0.0, vf)], axis=1
    ).astype(BF16)


def kernel(
    noise, n_pop, n_shard,
    tok_hbm, wg_hbm, wu_hbm, ag_hbm, au_hbm, hg_hbm, hu_hbm, fit_hbm, ro_hbm,
    sc_ref, left_hbm, right_hbm,
    tok, gath, hid, acc, total, ext, fac, ag, au, hg, hu, fit_ref, ro_ref, msg, abuf, left, parts,
    send, hsend, recv, wsem, lsem, asend, arecv, bsend, brecv, psend, precv, osem,
):
    pop, sh = lax.axis_index("pop"), lax.axis_index("shard")
    core, chip = pop % CORES, pop // CORES
    x, zh = chip % RING, chip // RING
    chunks = recv.shape[1] - 1
    chips = n_pop // CORES
    depth = wg_hbm.shape[0]
    rows = tok.shape[0]
    members = tok_hbm.shape[0]
    per_member = rows // members
    block = 2 * depth
    cols = chunks * LANES
    half_cols = cols // 2 // LANES * LANES + LANES
    span = CORES * depth

    def at(dx, dz):
        return (zh + dz) % 2 * RING + (x + dx) % RING

    def place(t, c, k=0):
        return (t * chips + c) * CORES + k

    def dev(c, k):
        return (c * CORES + k, sh)

    own, zown = at(0, 0), at(0, 1)
    xp, xm, xx = at(1, 0), at(3, 0), at(2, 0)
    zp, zm, zx = at(1, 1), at(3, 1), at(2, 1)

    def weight_load(t, k):
        src = (wg_hbm, wu_hbm)[k]
        col = pl.multiple_of(t * LANES, LANES)
        return pltpu.make_async_copy(
            src.at[:, pl.ds(col, LANES)],
            gath.at[place(t, own, core), pl.ds(k * depth, depth)], wsem.at[t],
        )

    small_loads = [
        pltpu.make_async_copy(a, b, lsem.at[i])
        for i, (a, b) in enumerate(((hg_hbm, hg), (hu_hbm, hu), (ag_hbm, ag), (au_hbm, au), (fit_hbm, fit_ref), (ro_hbm, ro_ref)))
    ]
    tok_loads = [
        pltpu.make_async_copy(
            tok_hbm.at[m], tok.at[pl.ds(m * per_member, per_member)], lsem.at[6 + m]
        )
        for m in range(members)
    ]
    for c in small_loads[:2]:
        c.start()

    @pl.loop(0, chunks)
    def _(t):
        weight_load(t, 0).start()
        weight_load(t, 1).start()

    for c in small_loads[2:] + tok_loads:
        c.start()

    barrier = pltpu.get_barrier_semaphore()

    @pl.loop(1, n_pop)
    def _(d):
        pl.semaphore_signal(barrier, inc=1, device_id=((pop + d) % n_pop, sh), device_id_type=MESH)

    @pl.loop(1, n_shard)
    def _(d):
        pl.semaphore_signal(barrier, inc=1, device_id=(pop, (sh + d) % n_shard), device_id_type=MESH)

    for c in small_loads[:2]:
        c.wait()

    def pack(gate, up):
        return jnp.concatenate(
            [gate[0].astype(F32), gate[1].astype(F32), up[0].astype(F32), up[1].astype(F32)], axis=0
        ).astype(BF16)

    hid[place(0, own, core)] = pack(hg, hu)

    pl.semaphore_wait(barrier, n_pop - 1 + n_shard - 1)

    def remote(kind, t, c, target, lo=0, n=block):
        ref = gath.at[place(t, c, core), pl.ds(lo, n)]
        return pltpu.make_async_remote_copy(
            src_ref=ref, dst_ref=ref, send_sem=send.at[0], recv_sem=recv.at[LANDS[kind], t],
            device_id=target, device_id_type=MESH,
        )

    to_z, to_p, to_m, to_s = dev(zown, core), dev(xp, core), dev(xm, core), dev(own, 1 - core)

    sends = {
        Z: (own, 0, block, to_z),
        A_LO: (own, 0, block, to_p), A_HI: (own, 0, block, to_m),
        B_LO: (zown, 0, block, to_p), B_HI: (zown, 0, block, to_m),
        RA_LO: (xm, 0, depth, to_p), RA_HI: (xp, depth, depth, to_m),
        RB_LO: (zm, depth, depth, to_p), RB_HI: (zp, 0, depth, to_m),
        S_OWN: (own, 0, block, to_s), S_Z: (zown, 0, block, to_s),
        S_A_LO: (xm, 0, block, to_s), S_A_HI: (xp, 0, block, to_s),
        S_B_LO: (zm, 0, block, to_s), S_B_HI: (zp, 0, block, to_s),
        S_RA: (xx, 0, block, to_s), S_RB: (zx, 0, block, to_s),
    }
    def put(kind, t):
        c, lo, n, target = sends[kind]
        remote(kind, t, c, target, lo, n).start()

    def put_factors(kind):
        c, lo, n, target = sends[kind]
        width = pl.ds(0, cols) if n == block else pl.ds(0, half_cols) if lo == 0 else pl.ds(half_cols, cols - half_cols)
        ref = hid.at[place(0, c, core), :, width]
        pltpu.make_async_remote_copy(
            src_ref=ref, dst_ref=ref, send_sem=hsend.at[0], recv_sem=recv.at[LANDS[kind], chunks],
            device_id=target, device_id_type=MESH,
        ).start()

    def got_factors(what):
        bulk(hid.at[pl.ds(0, BRINGS.get(what, 1))], hsend.at[0], recv.at[what, chunks]).wait_recv()

    def bulk(ref, send_sem, recv_sem):
        return pltpu.make_async_remote_copy(
            src_ref=ref, dst_ref=ref, send_sem=send_sem, recv_sem=recv_sem,
            device_id=to_s, device_id_type=MESH,
        )

    def got(what, t):
        bulk(gath.at[pl.ds(0, BRINGS.get(what, 1))], send.at[0], recv.at[what, t]).wait_recv()

    def open_chunk(t):
        both = gath.at[0, pl.ds(0, 2 * depth)]
        pltpu.make_async_copy(both, both, wsem.at[t]).wait()
        for kind in (A_LO, A_HI, S_OWN):
            put(kind, t)

    def pass_a(t):
        for what, relay, copy in ((W_A_LO, RA_LO, S_A_LO), (W_A_HI, RA_HI, S_A_HI)):
            got(what, t)
            put(relay, t)
            put(copy, t)

    open_chunk(0)
    put(Z, 0)
    open_chunk(1)

    for c in small_loads[2:]:
        c.wait()
    rank_rows = pack(ag, au)
    for k in range(3):
        fac[k * SMALL:(k + 1) * SMALL, :] = rank_rows
    fac[3 * SMALL:, :] = jnp.zeros((LANES - 3 * SMALL, fac.shape[1]), BF16)
    fit = fit_ref[...].astype(F32)
    row16 = lax.broadcasted_iota(jnp.int32, (SMALL, LANES), 0)
    f0 = jnp.broadcast_to(fit[:, 0:1], (SMALL, LANES))
    f1 = jnp.broadcast_to(fit[:, 1:2], (SMALL, LANES))
    fit_rows = jnp.where(row16 // 4 % 2 == 0, f0, f1).astype(BF16)
    for q in range(n_pop):
        msg[q, :, :depth] = rank_rows[:, q * depth:(q + 1) * depth]
        msg[q, :, depth:] = fit_rows

    def factor_copy(q):
        return pltpu.make_async_remote_copy(
            src_ref=msg.at[q], dst_ref=abuf.at[sh], send_sem=asend.at[0], recv_sem=arecv.at[0],
            device_id=(q, sh), device_id_type=MESH,
        )

    def spread_copy(target):
        return pltpu.make_async_remote_copy(
            src_ref=abuf.at[sh], dst_ref=abuf.at[sh], send_sem=bsend.at[0], recv_sem=brecv.at[0],
            device_id=(pop, target), device_id_type=MESH,
        )

    others = pl.ds(0, n_shard - 1)
    spread_all = bulk(abuf.at[others], bsend.at[0], brecv.at[0])

    @pl.when(pop == sh)
    def _():
        @pl.loop(1, n_pop)
        def _(d):
            factor_copy((pop + d) % n_pop).start()
        abuf[pop] = msg[pop]

    total[...] = jnp.zeros_like(total)

    def project():
        for c in tok_loads:
            c.wait()
        acc[0, :, :LANES] = jnp.zeros((rows, LANES), F32)

        @pl.loop(0, tok.shape[1] // span)
        def _(k):
            cols = pl.ds(pl.multiple_of(k * span, span), span)
            acc[0, :, :LANES] += dot(tok[:, cols], fac[:, cols], ((1,), (1,)))

        row = lax.broadcasted_iota(jnp.int32, (rows, LANES), 0)
        lane = lax.broadcasted_iota(jnp.int32, (rows, LANES), 1)
        mine = (row // per_member) == (lane // 4 % 2)
        p = jnp.where(mine, acc[0, :, :LANES] * noise, 0.0)
        hi, mid, lo = (v.astype(F32) for v in three_terms(p))
        group = lane // SMALL
        ext[...] = jnp.where(group == 0, hi, jnp.where(group == 1, mid, lo)).astype(BF16)

    def start_chunk(t, slot):
        rhs = split_rows(hid[place(0, own, core), :, pl.ds(pl.multiple_of(t * LANES, LANES), LANES)])
        pad = jnp.zeros((LANES - 3 * SMALL, 2 * LANES), BF16)
        acc[slot] = dot(ext[...], jnp.concatenate([rhs, rhs, rhs, pad], axis=0))

    def add_chip(t, slot, c):
        cols = pl.ds(pl.multiple_of(c * span, span), span)
        both = pl.ds(place(t, c), CORES)
        gate = gath[both, :depth, :].reshape(span, LANES)
        up = gath[both, depth:2 * depth, :].reshape(span, LANES)
        acc[slot] += dot(tok[:, cols], jnp.concatenate([gate, up], axis=1))

    def finish_chunk(t, slot):
        gate, up = acc[slot, :, :LANES], acc[slot, :, LANES:]
        hidden = gate / (1.0 + jnp.exp(-gate)) * up
        total[...] += hidden * ro_ref[pl.ds(t, 1), :]

    def build_left():
        a = abuf[:, :, :depth].reshape(n_pop * SMALL, depth).astype(F32)
        f = abuf[:, :, depth:].reshape(n_pop * SMALL, LANES).astype(F32)
        prod = a * jnp.concatenate([f] * (depth // LANES), axis=1)
        for k, part in enumerate(by_kind(prod, n_pop)):
            part = part.T
            hi = part.astype(BF16)
            n = part.shape[1]
            left[k, :, :n] = hi
            left[k, :, n:] = (part - hi.astype(F32)).astype(BF16)

    def left_out():
        return pltpu.make_async_copy(left, left_hbm, osem.at[1])

    def factor_out():
        return pltpu.make_async_copy(hid, right_hbm, osem.at[0])

    open_chunk(2)
    put(Z, 1)
    pass_a(0)

    @pl.loop(0, chunks + 2)
    def _(i):
        @pl.when(i + 3 < chunks)
        def _():
            open_chunk(i + 3)

        @pl.when(i + 1 < chunks)
        def _():
            pass_a(i + 1)

        @pl.when(i < chunks)
        def _():
            got(W_Z, i)
            for kind in (B_LO, B_HI):
                put(kind, i)

            @pl.when(i + 2 < chunks)
            def _():
                put(Z, i + 2)
            put(S_Z, i)

        @pl.when(i == chunks - 2)
        def _():
            put_factors(Z)

        @pl.when(i == chunks - 1)
        def _():
            for kind in (A_LO, A_HI, S_OWN):
                put_factors(kind)

        @pl.when((i >= 1) & (i < chunks + 1))
        def _():
            t = i - 1
            for what, relay, copy in ((W_B_LO, RB_LO, S_B_LO), (W_B_HI, RB_HI, S_B_HI)):
                got(what, t)
                put(relay, t)
                put(copy, t)

        @pl.when(i == chunks)
        def _():
            got_factors(W_Z)
            for kind in (B_LO, B_HI, S_Z):
                put_factors(kind)
            for what, relay, copy in ((W_A_LO, RA_LO, S_A_LO), (W_A_HI, RA_HI, S_A_HI)):
                got_factors(what)
                put_factors(relay)
                put_factors(copy)

        @pl.when((i >= 1) & (i < chunks + 1))
        def _():
            t = i - 1
            got(W_S_FIRST, t)
            start_chunk(t, t % 2)

            add_chip(t, t % 2, zown)

            @pl.loop(0, RING)
            def _(j):
                add_chip(t, t % 2, at(j, 0))

        @pl.when(i < chunks)
        def _():
            got(W_RA, i)
            put(S_RA, i)

        @pl.when(i >= 2)
        def _():
            got(W_RB, i - 2)
            put(S_RB, i - 2)

        @pl.when(i == chunks + 1)
        def _():
            for what, relay, copy in ((W_B_LO, RB_LO, S_B_LO), (W_B_HI, RB_HI, S_B_HI)):
                got_factors(what)
                put_factors(relay)
                put_factors(copy)
            got_factors(W_RA)
            put_factors(S_RA)

        @pl.when(i == 0)
        def _():
            project()

        @pl.when(i == 1)
        def _():
            @pl.when(pop != sh)
            def _():
                factor_copy(pop).wait_recv()

            @pl.loop(1, n_shard)
            def _(d):
                spread_copy((sh + d) % n_shard).start()

        @pl.when((i >= 1) & (i < chunks + 1))
        def _():
            t = i - 1
            got(W_S_B, t)

            @pl.loop(0, 2)
            def _(j):
                add_chip(t, t % 2, at(1 + 2 * j, 1))

        @pl.when(i >= 2)
        def _():
            got(W_S_RB, i - 2)
            add_chip(i - 2, i % 2, zx)
            finish_chunk(i - 2, i % 2)

        @pl.when(i == chunks - 1)
        def _():
            spread_all.wait_recv()
            build_left()
            left_out().start()

    ones = jnp.ones((SMALL, 3 * LANES), BF16)
    for m in range(members):
        part = dot(ones, jnp.concatenate(three_terms(total[m * per_member:(m + 1) * per_member, :]), axis=1), ((1,), (1,)))
        parts[sh, m:m + 1, :] = part[0:1, :]

    def score_copy(target):
        return pltpu.make_async_remote_copy(
            src_ref=parts.at[sh], dst_ref=parts.at[sh], send_sem=psend.at[0], recv_sem=precv.at[0],
            device_id=(pop, target), device_id_type=MESH,
        )

    @pl.loop(1, n_shard)
    def _(d):
        score_copy((sh + d) % n_shard).start()

    got_factors(W_RB)
    put_factors(S_RB)
    bulk(gath.at[pl.ds(0, chunks * BLOCKS)], send.at[0], recv.at[0, 0]).wait_send()
    for what in (W_S_FIRST, W_S_B, W_S_RB):
        got_factors(what)
    factor_out().start()
    bulk(hid.at[pl.ds(0, BLOCKS)], hsend.at[0], recv.at[0, 0]).wait_send()

    @pl.when(pop == sh)
    def _():
        bulk(msg.at[others], asend.at[0], arecv.at[0]).wait_send()

    spread_all.wait_send()
    left_out().wait()
    score_all = bulk(parts.at[others], psend.at[0], precv.at[0])
    score_all.wait_send()
    score_all.wait_recv()

    score = parts[0]
    for s in range(1, n_shard):
        score = score + parts[s]
    sc_ref[...] = score
    factor_out().wait()


def finish_kernel(out_scale, score_ref, left, right, sc_ref, ug_ref, uu_ref):
    sc_ref[...] = score_ref[...]
    n = right.shape[0]
    rows = by_kind(right[...].reshape(n * SMALL, right.shape[2]), n)
    for k, out in enumerate((ug_ref, uu_ref)):
        r = rows[k].astype(BF16)
        out[...] = dot(left[k], jnp.concatenate([r, r], axis=0)) * out_scale


def body(n_pop, n_shard, tokens, wg, wu, a_gate, a_up, h_gate, h_up, fitness, readout):
    members, tok_count, width = tokens.shape
    depth, cols = wg.shape
    ranks = a_gate.shape[1]
    chunks = cols // LANES
    rows = members * tok_count
    noise = 0.25 / math.sqrt(width * ranks)
    out_scale = 1.0 / math.sqrt(n_pop * members * ranks)
    block = 2 * depth
    dma = pltpu.SemaphoreType.DMA
    anyspec = pl.BlockSpec(memory_space=pl.ANY)
    vspec = pl.BlockSpec(memory_space=pltpu.VMEM)
    score, left, right = pl.pallas_call(
        functools.partial(kernel, noise, n_pop, n_shard),
        name="generation",
        out_shape=(
            jax.ShapeDtypeStruct((members, tok_count), F32),
            jax.ShapeDtypeStruct((2, depth, n_pop * SMALL), BF16),
            jax.ShapeDtypeStruct((n_pop, SMALL, cols), BF16),
        ),
        in_specs=[anyspec] * 9,
        out_specs=(vspec, anyspec, anyspec),
        scratch_shapes=[
            pltpu.VMEM((rows, width), BF16),
            pltpu.VMEM((chunks * n_pop, block, LANES), BF16),
            pltpu.VMEM((n_pop, SMALL, cols), BF16),
            pltpu.VMEM((2, rows, 2 * LANES), F32),
            pltpu.VMEM((rows, LANES), F32),
            pltpu.VMEM((rows, LANES), BF16),
            pltpu.VMEM((LANES, width), BF16),
            pltpu.VMEM((members, ranks, width), BF16),
            pltpu.VMEM((members, ranks, width), BF16),
            pltpu.VMEM((members, ranks, cols), BF16),
            pltpu.VMEM((members, ranks, cols), BF16),
            pltpu.VMEM((1, members), BF16),
            pltpu.VMEM((chunks, LANES), F32),
            pltpu.VMEM((n_pop, SMALL, depth + LANES), BF16),
            pltpu.VMEM((n_pop, SMALL, depth + LANES), BF16),
            pltpu.VMEM((2, depth, n_pop * SMALL), BF16),
            pltpu.VMEM((n_shard, members, tok_count), F32),
            dma((1,)), dma((1,)), dma((WAITS, chunks + 1)),
            dma((chunks,)), dma((8,)),
            dma((1,)), dma((1,)), dma((1,)), dma((1,)), dma((1,)), dma((1,)),
            dma((2,)),
        ],
        compiler_params=pltpu.CompilerParams(
            collective_id=0, has_side_effects=True, vmem_limit_bytes=56 * 1024 * 1024
        ),
    )(tokens, wg, wu, a_gate, a_up, h_gate, h_up, fitness.reshape(1, members), readout.reshape(chunks, LANES))
    return pl.pallas_call(
        functools.partial(finish_kernel, out_scale),
        name="updates",
        out_shape=(
            jax.ShapeDtypeStruct((members, tok_count), F32),
            jax.ShapeDtypeStruct((depth, cols), F32),
            jax.ShapeDtypeStruct((depth, cols), F32),
        ),
        grid=(2,),
        in_specs=[
            pl.BlockSpec((members, tok_count), lambda i: (0, 0)),
            pl.BlockSpec((2, depth // 2, n_pop * SMALL), lambda i: (0, i, 0)),
            pl.BlockSpec((n_pop, SMALL, cols), lambda i: (0, 0, 0)),
        ],
        out_specs=(
            pl.BlockSpec((members, tok_count), lambda i: (0, 0)),
            pl.BlockSpec((depth // 2, cols), lambda i: (i, 0)),
            pl.BlockSpec((depth // 2, cols), lambda i: (i, 0)),
        ),
    )(score, left, right)


def solution(mesh):
    placed = (
        P("pop", None, None),
        P("pop", "shard"),
        P("pop", "shard"),
        P("pop", None, None),
        P("pop", None, None),
        P("pop", None, "shard"),
        P("pop", None, "shard"),
        P("pop"),
        P("shard"),
    )
    return jax.shard_map(
        functools.partial(body, mesh.shape["pop"], mesh.shape["shard"]),
        mesh=mesh,
        in_specs=placed,
        out_specs=(P("pop", None), P("pop", "shard"), P("pop", "shard")),
        check_vma=False,
    )
```

```python
import functools
import math

import jax
import jax.numpy as jnp
from jax import lax
from jax.experimental import pallas as pl
from jax.experimental.pallas import tpu as pltpu
from jax.sharding import PartitionSpec as P

MESH = pl.DeviceIdType.MESH
F32 = jnp.float32
BF16 = jnp.bfloat16
LANES = 128
RING = 4
CORES = 2
SMALL = 16
(Z, A_LO, A_HI, B_LO, B_HI, RA_LO, RA_HI, RB_LO, RB_HI,
 S_OWN, S_Z, S_A_LO, S_A_HI, S_B_LO, S_B_HI, S_RA, S_RB) = range(17)
BLOCKS = 15
W_Z, W_A_LO, W_A_HI, W_B_LO, W_B_HI, W_RA, W_RB, W_S_FIRST, W_S_B, W_S_RB = range(10)
WAITS = 10
BRINGS = {W_S_FIRST: 5, W_S_B: 2}
LANDS = {
    Z: W_Z, A_LO: W_A_LO, A_HI: W_A_HI, B_LO: W_B_LO, B_HI: W_B_HI,
    RA_LO: W_RA, RA_HI: W_RA, RB_LO: W_RB, RB_HI: W_RB,
    S_OWN: W_S_FIRST, S_Z: W_S_FIRST, S_A_LO: W_S_FIRST, S_A_HI: W_S_FIRST, S_RA: W_S_FIRST,
    S_B_LO: W_S_B, S_B_HI: W_S_B, S_RB: W_S_RB,
}


def dot(a, b, dims=((1,), (0,)), precision=None):
    return lax.dot_general(a, b, (dims, ((), ())), precision=precision, preferred_element_type=F32)


def three_terms(v):
    hi = v.astype(BF16)
    rest = v - hi.astype(F32)
    mid = rest.astype(BF16)
    return hi, mid, (rest - mid.astype(F32)).astype(BF16)


def by_kind(v, n):
    v = v.astype(F32).reshape(n, SMALL, v.shape[-1])
    half = SMALL // 2
    return [v[:, k * half:(k + 1) * half].reshape(n * half, v.shape[-1]) for k in range(2)]


def split_rows(v):
    n = v.shape[0]
    gate_row = lax.broadcasted_iota(jnp.int32, (n, LANES), 0) % SMALL < SMALL // 2
    vf = v.astype(F32)
    return jnp.concatenate(
        [jnp.where(gate_row, vf, 0.0), jnp.where(gate_row, 0.0, vf)], axis=1
    ).astype(BF16)


def kernel(
    noise, n_pop, n_shard,
    tok_hbm, wg_hbm, wu_hbm, ag_hbm, au_hbm, hg_hbm, hu_hbm, fit_hbm, ro_hbm,
    sc_ref, left_hbm, right_hbm,
    tok, gath, hid, acc, total, ext, fac, ag, au, hg, hu, fit_ref, ro_ref, msg, abuf, left, parts,
    send, hsend, recv, wsem, lsem, asend, arecv, bsend, brecv, psend, precv, osem,
):
    pop, sh = lax.axis_index("pop"), lax.axis_index("shard")
    core, chip = pop % CORES, pop // CORES
    x, zh = chip % RING, chip // RING
    chunks = recv.shape[1] - 1
    chips = n_pop // CORES
    depth = wg_hbm.shape[0]
    rows = tok.shape[0]
    members = tok_hbm.shape[0]
    per_member = rows // members
    block = 2 * depth
    cols = chunks * LANES
    half_cols = cols // 2 // LANES * LANES + LANES
    span = CORES * depth

    def at(dx, dz):
        return (zh + dz) % 2 * RING + (x + dx) % RING

    def place(t, c, k=0):
        return (t * chips + c) * CORES + k

    def dev(c, k):
        return (c * CORES + k, sh)

    own, zown = at(0, 0), at(0, 1)
    xp, xm, xx = at(1, 0), at(3, 0), at(2, 0)
    zp, zm, zx = at(1, 1), at(3, 1), at(2, 1)

    def weight_load(t, k):
        src = (wg_hbm, wu_hbm)[k]
        col = pl.multiple_of(t * LANES, LANES)
        return pltpu.make_async_copy(
            src.at[:, pl.ds(col, LANES)],
            gath.at[place(t, own, core), pl.ds(k * depth, depth)], wsem.at[t],
        )

    small_loads = [
        pltpu.make_async_copy(a, b, lsem.at[i])
        for i, (a, b) in enumerate(((hg_hbm, hg), (hu_hbm, hu), (ag_hbm, ag), (au_hbm, au), (fit_hbm, fit_ref), (ro_hbm, ro_ref)))
    ]
    tok_loads = [
        pltpu.make_async_copy(
            tok_hbm.at[m], tok.at[pl.ds(m * per_member, per_member)], lsem.at[6 + m]
        )
        for m in range(members)
    ]
    for c in small_loads[:2]:
        c.start()

    @pl.loop(0, chunks)
    def _(t):
        weight_load(t, 0).start()
        weight_load(t, 1).start()

    for c in small_loads[2:] + tok_loads:
        c.start()

    barrier = pltpu.get_barrier_semaphore()

    @pl.loop(1, n_pop)
    def _(d):
        pl.semaphore_signal(barrier, inc=1, device_id=((pop + d) % n_pop, sh), device_id_type=MESH)

    @pl.loop(1, n_shard)
    def _(d):
        pl.semaphore_signal(barrier, inc=1, device_id=(pop, (sh + d) % n_shard), device_id_type=MESH)

    for c in small_loads[:2]:
        c.wait()

    def pack(gate, up):
        return jnp.concatenate(
            [gate[0].astype(F32), gate[1].astype(F32), up[0].astype(F32), up[1].astype(F32)], axis=0
        ).astype(BF16)

    hid[place(0, own, core)] = pack(hg, hu)

    pl.semaphore_wait(barrier, n_pop - 1 + n_shard - 1)

    def remote(kind, t, c, target, lo=0, n=block):
        ref = gath.at[place(t, c, core), pl.ds(lo, n)]
        return pltpu.make_async_remote_copy(
            src_ref=ref, dst_ref=ref, send_sem=send.at[0], recv_sem=recv.at[LANDS[kind], t],
            device_id=target, device_id_type=MESH,
        )

    to_z, to_p, to_m, to_s = dev(zown, core), dev(xp, core), dev(xm, core), dev(own, 1 - core)

    sends = {
        Z: (own, 0, block, to_z),
        A_LO: (own, 0, block, to_p), A_HI: (own, 0, block, to_m),
        B_LO: (zown, 0, block, to_p), B_HI: (zown, 0, block, to_m),
        RA_LO: (xm, 0, depth, to_p), RA_HI: (xp, depth, depth, to_m),
        RB_LO: (zm, depth, depth, to_p), RB_HI: (zp, 0, depth, to_m),
        S_OWN: (own, 0, block, to_s), S_Z: (zown, 0, block, to_s),
        S_A_LO: (xm, 0, block, to_s), S_A_HI: (xp, 0, block, to_s),
        S_B_LO: (zm, 0, block, to_s), S_B_HI: (zp, 0, block, to_s),
        S_RA: (xx, 0, block, to_s), S_RB: (zx, 0, block, to_s),
    }
    def put(kind, t):
        c, lo, n, target = sends[kind]
        remote(kind, t, c, target, lo, n).start()

    def put_factors(kind):
        c, lo, n, target = sends[kind]
        width = pl.ds(0, cols) if n == block else pl.ds(0, half_cols) if lo == 0 else pl.ds(half_cols, cols - half_cols)
        ref = hid.at[place(0, c, core), :, width]
        pltpu.make_async_remote_copy(
            src_ref=ref, dst_ref=ref, send_sem=hsend.at[0], recv_sem=recv.at[LANDS[kind], chunks],
            device_id=target, device_id_type=MESH,
        ).start()

    def got_factors(what):
        bulk(hid.at[pl.ds(0, BRINGS.get(what, 1))], hsend.at[0], recv.at[what, chunks]).wait_recv()

    def bulk(ref, send_sem, recv_sem):
        return pltpu.make_async_remote_copy(
            src_ref=ref, dst_ref=ref, send_sem=send_sem, recv_sem=recv_sem,
            device_id=to_s, device_id_type=MESH,
        )

    def got(what, t):
        bulk(gath.at[pl.ds(0, BRINGS.get(what, 1))], send.at[0], recv.at[what, t]).wait_recv()

    def open_chunk(t):
        both = gath.at[0, pl.ds(0, 2 * depth)]
        pltpu.make_async_copy(both, both, wsem.at[t]).wait()
        for kind in (A_LO, A_HI, S_OWN):
            put(kind, t)

    def pass_a(t):
        for what, relay, copy in ((W_A_LO, RA_LO, S_A_LO), (W_A_HI, RA_HI, S_A_HI)):
            got(what, t)
            put(relay, t)
            put(copy, t)

    open_chunk(0)
    put(Z, 0)
    open_chunk(1)

    for c in small_loads[2:]:
        c.wait()
    rank_rows = pack(ag, au)
    for k in range(3):
        fac[k * SMALL:(k + 1) * SMALL, :] = rank_rows
    fac[3 * SMALL:, :] = jnp.zeros((LANES - 3 * SMALL, fac.shape[1]), BF16)
    fit = fit_ref[...].astype(F32)
    row16 = lax.broadcasted_iota(jnp.int32, (SMALL, LANES), 0)
    f0 = jnp.broadcast_to(fit[:, 0:1], (SMALL, LANES))
    f1 = jnp.broadcast_to(fit[:, 1:2], (SMALL, LANES))
    fit_rows = jnp.where(row16 // 4 % 2 == 0, f0, f1).astype(BF16)
    for q in range(n_pop):
        msg[q, :, :depth] = rank_rows[:, q * depth:(q + 1) * depth]
        msg[q, :, depth:] = fit_rows

    def factor_copy(q):
        return pltpu.make_async_remote_copy(
            src_ref=msg.at[q], dst_ref=abuf.at[sh], send_sem=asend.at[0], recv_sem=arecv.at[0],
            device_id=(q, sh), device_id_type=MESH,
        )

    def spread_copy(target):
        return pltpu.make_async_remote_copy(
            src_ref=abuf.at[sh], dst_ref=abuf.at[sh], send_sem=bsend.at[0], recv_sem=brecv.at[0],
            device_id=(pop, target), device_id_type=MESH,
        )

    others = pl.ds(0, n_shard - 1)
    spread_all = bulk(abuf.at[others], bsend.at[0], brecv.at[0])

    @pl.when(pop == sh)
    def _():
        @pl.loop(1, n_pop)
        def _(d):
            factor_copy((pop + d) % n_pop).start()
        abuf[pop] = msg[pop]

    total[...] = jnp.zeros_like(total)

    def project():
        for c in tok_loads:
            c.wait()
        acc[0, :, :LANES] = jnp.zeros((rows, LANES), F32)

        @pl.loop(0, tok.shape[1] // span)
        def _(k):
            cols = pl.ds(pl.multiple_of(k * span, span), span)
            acc[0, :, :LANES] += dot(tok[:, cols], fac[:, cols], ((1,), (1,)))

        row = lax.broadcasted_iota(jnp.int32, (rows, LANES), 0)
        lane = lax.broadcasted_iota(jnp.int32, (rows, LANES), 1)
        mine = (row // per_member) == (lane // 4 % 2)
        p = jnp.where(mine, acc[0, :, :LANES] * noise, 0.0)
        hi, mid, lo = (v.astype(F32) for v in three_terms(p))
        group = lane // SMALL
        ext[...] = jnp.where(group == 0, hi, jnp.where(group == 1, mid, lo)).astype(BF16)

    def start_chunk(t, slot):
        rhs = split_rows(hid[place(0, own, core), :, pl.ds(pl.multiple_of(t * LANES, LANES), LANES)])
        pad = jnp.zeros((LANES - 3 * SMALL, 2 * LANES), BF16)
        acc[slot] = dot(ext[...], jnp.concatenate([rhs, rhs, rhs, pad], axis=0))

    def add_chip(t, slot, c):
        cols = pl.ds(pl.multiple_of(c * span, span), span)
        both = pl.ds(place(t, c), CORES)
        gate = gath[both, :depth, :].reshape(span, LANES)
        up = gath[both, depth:2 * depth, :].reshape(span, LANES)
        acc[slot] += dot(tok[:, cols], jnp.concatenate([gate, up], axis=1))

    def finish_chunk(t, slot):
        gate, up = acc[slot, :, :LANES], acc[slot, :, LANES:]
        hidden = gate / (1.0 + jnp.exp(-gate)) * up
        total[...] += hidden * ro_ref[pl.ds(t, 1), :]

    def build_left():
        a = abuf[:, :, :depth].reshape(n_pop * SMALL, depth).astype(F32)
        f = abuf[:, :, depth:].reshape(n_pop * SMALL, LANES).astype(F32)
        prod = a * jnp.concatenate([f] * (depth // LANES), axis=1)
        for k, part in enumerate(by_kind(prod, n_pop)):
            part = part.T
            hi = part.astype(BF16)
            n = part.shape[1]
            left[k, :, :n] = hi
            left[k, :, n:] = (part - hi.astype(F32)).astype(BF16)

    def left_out():
        return pltpu.make_async_copy(left, left_hbm, osem.at[1])

    def factor_out():
        return pltpu.make_async_copy(hid, right_hbm, osem.at[0])

    open_chunk(2)
    put(Z, 1)
    pass_a(0)

    @pl.loop(0, chunks + 2)
    def _(i):
        @pl.when(i + 3 < chunks)
        def _():
            open_chunk(i + 3)

        @pl.when(i + 1 < chunks)
        def _():
            pass_a(i + 1)

        @pl.when(i < chunks)
        def _():
            got(W_Z, i)
            for kind in (B_LO, B_HI):
                put(kind, i)

            @pl.when(i + 2 < chunks)
            def _():
                put(Z, i + 2)
            put(S_Z, i)

        @pl.when(i == chunks - 2)
        def _():
            put_factors(Z)

        @pl.when(i == chunks - 1)
        def _():
            for kind in (A_LO, A_HI, S_OWN):
                put_factors(kind)

        @pl.when((i >= 1) & (i < chunks + 1))
        def _():
            t = i - 1
            for what, relay, copy in ((W_B_LO, RB_LO, S_B_LO), (W_B_HI, RB_HI, S_B_HI)):
                got(what, t)
                put(relay, t)
                put(copy, t)

        @pl.when((i >= 1) & (i < chunks + 1))
        def _():
            t = i - 1
            got(W_S_FIRST, t)
            start_chunk(t, t % 2)

            add_chip(t, t % 2, zown)

            @pl.loop(0, RING)
            def _(j):
                add_chip(t, t % 2, at(j, 0))

        @pl.when(i == chunks)
        def _():
            got_factors(W_Z)
            for kind in (B_LO, B_HI, S_Z):
                put_factors(kind)
            for what, relay, copy in ((W_A_LO, RA_LO, S_A_LO), (W_A_HI, RA_HI, S_A_HI)):
                got_factors(what)
                put_factors(relay)
                put_factors(copy)

        @pl.when(i < chunks)
        def _():
            got(W_RA, i)
            put(S_RA, i)

        @pl.when(i >= 2)
        def _():
            got(W_RB, i - 2)
            put(S_RB, i - 2)

        @pl.when(i == chunks + 1)
        def _():
            for what, relay, copy in ((W_B_LO, RB_LO, S_B_LO), (W_B_HI, RB_HI, S_B_HI)):
                got_factors(what)
                put_factors(relay)
                put_factors(copy)
            got_factors(W_RA)
            put_factors(S_RA)

        @pl.when(i == 0)
        def _():
            project()

        @pl.when(i == 1)
        def _():
            @pl.when(pop != sh)
            def _():
                factor_copy(pop).wait_recv()

            @pl.loop(1, n_shard)
            def _(d):
                spread_copy((sh + d) % n_shard).start()

        @pl.when((i >= 1) & (i < chunks + 1))
        def _():
            t = i - 1
            got(W_S_B, t)

            @pl.loop(0, 2)
            def _(j):
                add_chip(t, t % 2, at(1 + 2 * j, 1))

        @pl.when(i >= 2)
        def _():
            got(W_S_RB, i - 2)
            add_chip(i - 2, i % 2, zx)
            finish_chunk(i - 2, i % 2)

        @pl.when(i == chunks - 1)
        def _():
            spread_all.wait_recv()
            build_left()
            left_out().start()

    ones = jnp.ones((SMALL, 3 * LANES), BF16)
    for m in range(members):
        part = dot(ones, jnp.concatenate(three_terms(total[m * per_member:(m + 1) * per_member, :]), axis=1), ((1,), (1,)))
        parts[sh, m:m + 1, :] = part[0:1, :]

    def score_copy(target):
        return pltpu.make_async_remote_copy(
            src_ref=parts.at[sh], dst_ref=parts.at[sh], send_sem=psend.at[0], recv_sem=precv.at[0],
            device_id=(pop, target), device_id_type=MESH,
        )

    @pl.loop(1, n_shard)
    def _(d):
        score_copy((sh + d) % n_shard).start()

    got_factors(W_RB)
    put_factors(S_RB)
    bulk(gath.at[pl.ds(0, chunks * BLOCKS)], send.at[0], recv.at[0, 0]).wait_send()
    for what in (W_S_FIRST, W_S_B, W_S_RB):
        got_factors(what)
    factor_out().start()
    bulk(hid.at[pl.ds(0, BLOCKS)], hsend.at[0], recv.at[0, 0]).wait_send()

    @pl.when(pop == sh)
    def _():
        bulk(msg.at[others], asend.at[0], arecv.at[0]).wait_send()

    spread_all.wait_send()
    left_out().wait()
    score_all = bulk(parts.at[others], psend.at[0], precv.at[0])
    score_all.wait_send()
    score_all.wait_recv()

    score = parts[0]
    for s in range(1, n_shard):
        score = score + parts[s]
    sc_ref[...] = score
    factor_out().wait()


def finish_kernel(out_scale, score_ref, left, right, sc_ref, ug_ref, uu_ref):
    sc_ref[...] = score_ref[...]
    n = right.shape[0]
    rows = by_kind(right[...].reshape(n * SMALL, right.shape[2]), n)
    for k, out in enumerate((ug_ref, uu_ref)):
        r = rows[k].astype(BF16)
        out[...] = dot(left[k], jnp.concatenate([r, r], axis=0)) * out_scale


def body(n_pop, n_shard, tokens, wg, wu, a_gate, a_up, h_gate, h_up, fitness, readout):
    members, tok_count, width = tokens.shape
    depth, cols = wg.shape
    ranks = a_gate.shape[1]
    chunks = cols // LANES
    rows = members * tok_count
    noise = 0.25 / math.sqrt(width * ranks)
    out_scale = 1.0 / math.sqrt(n_pop * members * ranks)
    block = 2 * depth
    dma = pltpu.SemaphoreType.DMA
    anyspec = pl.BlockSpec(memory_space=pl.ANY)
    vspec = pl.BlockSpec(memory_space=pltpu.VMEM)
    score, left, right = pl.pallas_call(
        functools.partial(kernel, noise, n_pop, n_shard),
        name="generation",
        out_shape=(
            jax.ShapeDtypeStruct((members, tok_count), F32),
            jax.ShapeDtypeStruct((2, depth, n_pop * SMALL), BF16),
            jax.ShapeDtypeStruct((n_pop, SMALL, cols), BF16),
        ),
        in_specs=[anyspec] * 9,
        out_specs=(vspec, anyspec, anyspec),
        scratch_shapes=[
            pltpu.VMEM((rows, width), BF16),
            pltpu.VMEM((chunks * n_pop, block, LANES), BF16),
            pltpu.VMEM((n_pop, SMALL, cols), BF16),
            pltpu.VMEM((2, rows, 2 * LANES), F32),
            pltpu.VMEM((rows, LANES), F32),
            pltpu.VMEM((rows, LANES), BF16),
            pltpu.VMEM((LANES, width), BF16),
            pltpu.VMEM((members, ranks, width), BF16),
            pltpu.VMEM((members, ranks, width), BF16),
            pltpu.VMEM((members, ranks, cols), BF16),
            pltpu.VMEM((members, ranks, cols), BF16),
            pltpu.VMEM((1, members), BF16),
            pltpu.VMEM((chunks, LANES), F32),
            pltpu.VMEM((n_pop, SMALL, depth + LANES), BF16),
            pltpu.VMEM((n_pop, SMALL, depth + LANES), BF16),
            pltpu.VMEM((2, depth, n_pop * SMALL), BF16),
            pltpu.VMEM((n_shard, members, tok_count), F32),
            dma((1,)), dma((1,)), dma((WAITS, chunks + 1)),
            dma((chunks,)), dma((8,)),
            dma((1,)), dma((1,)), dma((1,)), dma((1,)), dma((1,)), dma((1,)),
            dma((2,)),
        ],
        compiler_params=pltpu.CompilerParams(
            collective_id=0, has_side_effects=True, vmem_limit_bytes=56 * 1024 * 1024
        ),
    )(tokens, wg, wu, a_gate, a_up, h_gate, h_up, fitness.reshape(1, members), readout.reshape(chunks, LANES))
    return pl.pallas_call(
        functools.partial(finish_kernel, out_scale),
        name="updates",
        out_shape=(
            jax.ShapeDtypeStruct((members, tok_count), F32),
            jax.ShapeDtypeStruct((depth, cols), F32),
            jax.ShapeDtypeStruct((depth, cols), F32),
        ),
        grid=(2,),
        in_specs=[
            pl.BlockSpec((members, tok_count), lambda i: (0, 0)),
            pl.BlockSpec((2, depth // 2, n_pop * SMALL), lambda i: (0, i, 0)),
            pl.BlockSpec((n_pop, SMALL, cols), lambda i: (0, 0, 0)),
        ],
        out_specs=(
            pl.BlockSpec((members, tok_count), lambda i: (0, 0)),
            pl.BlockSpec((depth // 2, cols), lambda i: (i, 0)),
            pl.BlockSpec((depth // 2, cols), lambda i: (i, 0)),
        ),
    )(score, left, right)


def solution(mesh):
    placed = (
        P("pop", None, None),
        P("pop", "shard"),
        P("pop", "shard"),
        P("pop", None, None),
        P("pop", None, None),
        P("pop", None, "shard"),
        P("pop", None, "shard"),
        P("pop"),
        P("shard"),
    )
    return jax.shard_map(
        functools.partial(body, mesh.shape["pop"], mesh.shape["shard"]),
        mesh=mesh,
        in_specs=placed,
        out_specs=(P("pop", None), P("pop", "shard"), P("pop", "shard")),
        check_vma=False,
    )
```
